32 devices in a mesh: gx: 8 (over y, x, core), gy: 4 (over z).
Axes of the slice: x: 2, y: 2, z: 4, core: 2. Of those that a mesh axis runs over, the one named last changes fastest.
Arguments:
- x_first: bfloat16 [128, 16384], P(None, 'gx'), may hold values from -160 to 160
- x_second: bfloat16 [128, 16384], P(None, 'gx'), may hold values from -160 to 160
- norm_gain: bfloat16 [16384], P('gx'), may hold values from 0.25 to 1.75
- w_qkv: bfloat16 [16384, 18432], P('gx', 'gy'), may hold values from -0.046875 to 0.046875
- w_out: bfloat16 [16384, 16384], P('gy', 'gx'), may hold values from -0.046875 to 0.046875
- cache_keys: bfloat16 [128, 768, 1024], P(('gx', 'gy')), may hold values from -240 to 240
- cache_values: bfloat16 [128, 768, 1024], P(('gx', 'gy')), may hold values from -8 to 8
- lengths: int32 [128], P(('gx', 'gy')), may hold values from 1 to 768, as said below
Outputs:
- out_first: bfloat16 [128, 16384], P('gy', 'gx')
- out_second: bfloat16 [128, 16384], P('gy', 'gx')
The draws below stay inside these ranges and needn't reach their ends.
Inputs may be any that keep to these rules, and one draw needn't show every extreme that they name: `lengths`: some sequence has exactly 768 filled slots in every draw.
All inputs are finite; a program needn't handle non-finite values.
Results may differ from the reference program's by a relative error of at most 0.012.
The reference program's roundings to bfloat16 on the way count: a program that leaves them out, or rounds other values in their place, can miss the bound.
Values may be sent and summed in bfloat16 or wider, within the bound.
A program may use at most 192 MiB of HBM per device.

```python
import math
import jax
import jax.numpy as jnp
from jax import lax

D = 16384
HEADS = 128
KVH = 8
HD = 128
CACHE = 768
BATCH = 128
GROUP = 16


def draw_inputs(key, salt):
    key = jax.random.fold_in(key, salt)
    noise_key, column_key, row_key = jax.random.split(key, 3)
    noise = jnp.clip(jax.random.normal(noise_key, (BATCH, D), jnp.float32), -4.0, 4.0)
    rise = 3.0
    column = jnp.arange(D, dtype=jnp.float32) / D
    column_scale = rise ** column * jnp.exp(jax.random.uniform(column_key, (D,), jnp.float32, 0.0, math.log(3.3)))
    row_scale = jnp.exp(jax.random.uniform(row_key, (BATCH, 1), jnp.float32, math.log(0.3), math.log(3.0)))
    return (noise * column_scale[None, :] * row_scale).astype(jnp.bfloat16)


def draw_x_first(key, part):
    return draw_inputs(key, 101)


def draw_x_second(key, part):
    return draw_inputs(key, 202)


def draw_cache_keys(key, part):
    key = jax.random.fold_in(key, 303)
    noise_key = jax.random.fold_in(key, 0)
    noise = jnp.clip(jax.random.normal(noise_key, (BATCH, CACHE, KVH * HD), jnp.float32), -4.0, 4.0)
    return noise.astype(jnp.bfloat16)


def draw_cache_values(key, part):
    key = jax.random.fold_in(key, 404)
    offset_key, noise_key = jax.random.split(key)
    offset = jnp.clip(jax.random.normal(offset_key, (BATCH, 1, KVH * HD), jnp.float32), -4.0, 4.0)
    noise = jnp.clip(jax.random.normal(noise_key, (BATCH, CACHE, KVH * HD), jnp.float32), -4.0, 4.0)
    return (offset + noise).astype(jnp.bfloat16)


def draw_lengths(key, part):
    key = jax.random.fold_in(key, 505)
    first_key, second_key, third_key, pick_key = jax.random.split(key, 4)
    first = jax.random.randint(first_key, (BATCH,), 1, CACHE + 1)
    second = jax.random.randint(second_key, (BATCH,), 1, CACHE + 1)
    third = jax.random.randint(third_key, (BATCH,), 1, CACHE + 1)
    shortest = jnp.minimum(jnp.minimum(first, second), third)
    chosen = jax.random.randint(pick_key, (), 0, BATCH)
    return jnp.where(jnp.arange(BATCH, dtype=jnp.int32) == chosen, CACHE, shortest).astype(jnp.int32)


def shard_levels(rng, shape, shards, least, high):
    def one(dim, parts):
        steps = jax.random.uniform(jax.random.fold_in(jax.random.fold_in(rng, 6), dim), (parts,), jnp.float32, least / len(shards), high / len(shards))
        return jnp.repeat(jnp.exp(steps), shape[dim] // parts).reshape((-1,) + (1,) * (len(shape) - dim - 1))

    loudness = one(*shards[0])
    for cut in shards[1:]:
        loudness = loudness * one(*cut)
    return loudness


def centred(rng, shape, deviation, bound, shards=(), kind=jnp.bfloat16):
    result = jax.random.normal(rng, shape, jnp.float32) * deviation
    if len(shards) > 0:
        result = shard_levels(rng, shape, shards, -0.22, 0.18) * result
    return jnp.clip(result, min=-bound, max=bound).astype(kind)


def setup_inputs(seed: int = 0) -> dict:
    key_list = jax.random.split(jax.random.key(seed), 9)
    return {
        "x_first": draw_x_first(jax.random.fold_in(key_list[8], 71), 0),
        "x_second": draw_x_second(jax.random.fold_in(key_list[8], 71), 0),
        "norm_gain": jnp.clip(1.0 + 0.15 * jax.random.normal(key_list[2], (D,), jnp.float32), 0.25, 1.75).astype(jnp.bfloat16),
        "w_qkv": centred(key_list[3], (D, (HEADS + 2 * KVH) * HD), D ** -0.5, 0.046875, ((0, 8), (1, 4))),
        "w_out": centred(key_list[4], (HEADS * HD, D), (HEADS * HD) ** -0.5, 0.046875, ((0, 4), (1, 8))),
        "cache_keys": draw_cache_keys(jax.random.fold_in(key_list[8], 71), 0),
        "cache_values": draw_cache_values(jax.random.fold_in(key_list[8], 71), 0),
        "lengths": draw_lengths(jax.random.fold_in(key_list[8], 71), 0),
    }


norm_eps = 1e-05
rotary_base = 500000.0

def rotate_pairs(values, position):
    half_width = values.shape[-1] // 2
    freq = rotary_base ** (-(jnp.arange(half_width, dtype=jnp.float32) * 2.0 / values.shape[-1]))
    angle = position.astype(jnp.float32)[..., None] * freq
    shape = position.shape + (1,) * (values.ndim - position.ndim - 1) + (half_width,)
    cosine = jnp.cos(angle).reshape(shape)
    sine = jnp.sin(angle).reshape(shape)
    first = values[..., :half_width]
    second = values[..., half_width:]
    return jnp.concatenate([first * cosine - second * sine, second * cosine + first * sine], axis=-1)

def project(x_rows, norm_gain, w_qkv):
    wide = x_rows.astype(jnp.float32)
    squares = lax.optimization_barrier(jnp.sum(wide * wide, axis=1))
    row_scale = lax.rsqrt(squares / D + norm_eps)
    scaled = (wide * norm_gain.astype(jnp.float32)[None, :]).astype(jnp.bfloat16)
    partial_sum = jnp.dot(scaled, w_qkv, preferred_element_type=jnp.float32)
    joined = (partial_sum * row_scale[:, None]).astype(jnp.bfloat16)
    joined = joined.reshape(BATCH, KVH, GROUP + 2, HD)
    return (joined[:, :, :GROUP], joined[:, :, GROUP], joined[:, :, GROUP + 1])

def attend_row(packed):
    query, keys_cache, values_cache, length, extra_keys, extra_values = packed
    score_scale = 1.0 / math.sqrt(HD)
    query_wide = query.astype(jnp.float32)
    keys_wide = keys_cache.astype(jnp.float32).reshape(CACHE, KVH, HD)
    values_wide = values_cache.astype(jnp.float32).reshape(CACHE, KVH, HD)
    cache_scores = jnp.einsum('kgd,tkd->kgt', query_wide, keys_wide) * score_scale
    valid = jnp.arange(CACHE, dtype=jnp.int32) < length
    cache_scores = jnp.where(valid[None, None, :], cache_scores, -jnp.inf)
    extra_scores = jnp.einsum('kgd,ekd->kge', query_wide, extra_keys.astype(jnp.float32)) * score_scale
    top = jnp.maximum(lax.optimization_barrier(jnp.max(cache_scores, axis=-1)), lax.optimization_barrier(jnp.max(extra_scores, axis=-1)))[..., None]
    cache_weights = jnp.exp(cache_scores - top)
    extra_weights = jnp.exp(extra_scores - top)
    total = lax.optimization_barrier(jnp.sum(cache_weights, axis=-1)) + lax.optimization_barrier(jnp.sum(extra_weights, axis=-1))
    cache_round = lax.optimization_barrier(cache_weights.astype(jnp.bfloat16)).astype(jnp.float32)
    extra_round = lax.optimization_barrier(extra_weights.astype(jnp.bfloat16)).astype(jnp.float32)
    mixed = jnp.einsum('kgt,tkd->kgd', cache_round, values_wide)
    mixed = mixed + jnp.einsum('kge,ekd->kgd', extra_round, extra_values.astype(jnp.float32))
    return (mixed / total[..., None]).astype(jnp.bfloat16).reshape(HEADS * HD)

def reference(x_first, x_second, norm_gain, w_qkv, w_out, cache_keys, cache_values, lengths):
    query_one, key_one, value_one = project(x_first, norm_gain, w_qkv)
    query_two, key_two, value_two = project(x_second, norm_gain, w_qkv)
    position_one = lengths
    position_two = lengths + 1
    query_one = rotate_pairs(query_one.astype(jnp.float32), position_one).astype(jnp.bfloat16)
    key_one = rotate_pairs(key_one.astype(jnp.float32), position_one).astype(jnp.bfloat16)
    query_two = rotate_pairs(query_two.astype(jnp.float32), position_two).astype(jnp.bfloat16)
    key_two = rotate_pairs(key_two.astype(jnp.float32), position_two).astype(jnp.bfloat16)
    heads_one = lax.map(attend_row, (query_one, cache_keys, cache_values, lengths, key_one[:, None], value_one[:, None]))
    keys_both = jnp.stack([key_one, key_two], axis=1)
    values_both = jnp.stack([value_one, value_two], axis=1)
    heads_two = lax.map(attend_row, (query_two, cache_keys, cache_values, lengths, keys_both, values_both))
    out_first = jnp.dot(heads_one, w_out, preferred_element_type=jnp.float32).astype(jnp.bfloat16)
    out_second = jnp.dot(heads_two, w_out, preferred_element_type=jnp.float32).astype(jnp.bfloat16)
    return (out_first, out_second)
```

```python
import functools
import math

import jax
import jax.numpy as jnp
from jax import lax
from jax.experimental import pallas as pl
from jax.experimental.pallas import tpu as pltpu
from jax.sharding import PartitionSpec as P

HD = 128
norm_eps = 1e-05
rotary_base = 500000.0
STEPS = 2
VMEM_LIMIT = 60 * 1024 * 1024


MESH = pl.DeviceIdType.MESH


def signal_peers(peers):
    barrier = pltpu.get_barrier_semaphore()
    for peer in peers:
        pl.semaphore_signal(barrier, inc=1, device_id=peer, device_id_type=MESH)
    pl.semaphore_wait(barrier, len(peers))


def places(outer, inner):
    gx, gy = lax.axis_index("gx"), lax.axis_index("gy")
    pairs = outer // 2
    pair, side = gx // 2, lax.rem(gx, 2)
    other = (gx + 1 - 2 * side, gy)
    along = [(2 * lax.rem(pair + d, pairs) + side, gy) for d in range(1, pairs)]
    across = [(gx, lax.rem(gy + d, inner)) for d in range(1, inner)]
    return gx, gy, pair, side, other, along, across


def project_kernel(
    dims, x_first, x_second, gain, w, out,
    scaled, w_here, prod, from_other, to_along, from_along, sq, sq_other, sq_to, sq_along,
    mixed, to_across, w_sem, pair_send, pair_recv, along_send, along_recv, across_send,
    across_recv, sq_send, sq_recv, sqa_send, sqa_recv, own_sem,
):
    outer, inner, rows, width, chunk_heads, chunks = dims
    gx, gy, pair, side, other, along, across = places(outer, inner)
    pairs = outer // 2
    cw = chunk_heads * HD
    block = inner * rows
    tile = STEPS * rows

    def w_copy(n):
        return pltpu.make_async_copy(w.at[:, pl.ds(n * cw, cw)], w_here.at[n], w_sem.at[n])

    for n in range(chunks):
        w_copy(n).start()
    signal_peers([other] + along + across)

    wide_gain = gain[...].astype(jnp.float32)
    for s, x in enumerate((x_first, x_second)):

        @pl.loop(0, outer)
        def _(g):
            wide = x[pl.ds(g * block, block), :].astype(jnp.float32)
            row = g * STEPS * block + s * block
            scaled[pl.ds(row, block), :] = (wide * wide_gain).astype(jnp.bfloat16)
            total = jnp.sum(wide * wide, axis=1, keepdims=True)
            sq[g // 2, g % 2, s * block : (s + 1) * block, :] = jnp.broadcast_to(
                total, (block, HD)
            )

    def send_sq():
        return pltpu.make_async_remote_copy(
            src_ref=sq.at[:, 1 - side], dst_ref=sq_other, send_sem=sq_send, recv_sem=sq_recv,
            device_id=other, device_id_type=MESH,
        )

    def send_pair(n):
        return pltpu.make_async_remote_copy(
            src_ref=prod.at[n, :, 1 - side], dst_ref=from_other.at[n],
            send_sem=pair_send.at[n], recv_sem=pair_recv.at[n],
            device_id=other, device_id_type=MESH,
        )

    def send_along(n, d):
        return pltpu.make_async_remote_copy(
            src_ref=to_along.at[n, d], dst_ref=from_along.at[n, d],
            send_sem=along_send.at[n, d], recv_sem=along_recv.at[n, d],
            device_id=along[d], device_id_type=MESH,
        )

    def send_sq_along(d):
        return pltpu.make_async_remote_copy(
            src_ref=sq_to.at[d], dst_ref=sq_along.at[d],
            send_sem=sqa_send.at[d], recv_sem=sqa_recv.at[d],
            device_id=along[d], device_id_type=MESH,
        )

    def send_across(n, d):
        return pltpu.make_async_remote_copy(
            src_ref=to_across.at[n, lax.rem(gy + d + 1, inner)],
            dst_ref=out.at[gy, pl.ds(n * chunk_heads, chunk_heads)],
            send_sem=across_send.at[n, d], recv_sem=across_recv.at[n, d],
            device_id=across[d], device_id_type=MESH,
        )

    def keep_own(n):
        return pltpu.make_async_copy(
            to_across.at[n, gy], out.at[gy, pl.ds(n * chunk_heads, chunk_heads)], own_sem.at[n]
        )

    send_sq().start()

    def pass_on(n):
        send_pair(n).wait()
        for d in range(pairs - 1):
            there = lax.rem(pair + d + 1, pairs)
            to_along[n, d] = (prod[n, there, side] + from_other[n, there]).astype(jnp.bfloat16)
            send_along(n, d).start()

    @pl.loop(0, chunks)
    def _(n):
        w_copy(n).wait()
        product = jnp.dot(scaled[...], w_here[n], preferred_element_type=jnp.float32)
        prod[n] = product.reshape(pairs, 2, STEPS * block, cw)
        send_pair(n).start()

        @pl.when(n == 0)
        def _():
            send_sq().wait()
            for d in range(pairs - 1):
                there = lax.rem(pair + d + 1, pairs)
                sq_to[d] = sq[there, side] + sq_other[there]
                send_sq_along(d).start()

        @pl.when(n > 0)
        def _():
            pass_on(n - 1)

    pass_on(chunks - 1)

    squares = sq[pair, side] + sq_other[pair]
    for d in range(pairs - 1):
        send_sq_along(d).wait()
        squares = squares + sq_along[d]
    factor = lax.rsqrt(squares / width + norm_eps)
    sq[0, 0] = factor

    @pl.loop(0, chunks)
    def _(n):
        for d in range(pairs - 1):
            send_along(n, d).wait()
        for h in range(chunk_heads):
            columns = slice(h * HD, (h + 1) * HD)
            total = prod[n, pair, side, :, columns] + from_other[n, pair, :, columns]
            for d in range(pairs - 1):
                total = total + from_along[n, d, :, columns].astype(jnp.float32)
            total = total * sq[0, 0]
            for s in range(STEPS):
                for z in range(inner):
                    mixed[h, z * tile + s * rows : z * tile + (s + 1) * rows, :] = total[
                        s * block + z * rows : s * block + (z + 1) * rows
                    ]
            for z in range(inner):
                to_across[n, z, h] = mixed[h, z * tile : (z + 1) * tile, :].astype(jnp.bfloat16)
        for d in range(inner - 1):
            send_across(n, d).start()
        keep_own(n).start()

    @pl.loop(0, chunks)
    def _(n):
        keep_own(n).wait()
        for d in range(inner - 1):
            send_across(n, d).wait()


def project(x_first, x_second, gain, w, outer, inner, rows, width):
    depth, columns = w.shape
    heads = columns // HD
    chunk_heads = 6
    chunks = heads // chunk_heads
    cw = chunk_heads * HD
    pairs = outer // 2
    here = STEPS * inner * rows
    tile = STEPS * rows
    dims = (outer, inner, rows, width, chunk_heads, chunks)
    dma = pltpu.SemaphoreType.DMA
    vmem = pl.BlockSpec(memory_space=pltpu.VMEM)
    f32, b16 = jnp.float32, jnp.bfloat16
    return pl.pallas_call(
        functools.partial(project_kernel, dims),
        in_specs=[vmem, vmem, vmem, pl.BlockSpec(memory_space=pl.ANY)],
        out_specs=vmem,
        out_shape=jax.ShapeDtypeStruct((inner, heads, tile, HD), b16),
        scratch_shapes=[
            pltpu.VMEM((outer * here, depth), b16),
            pltpu.VMEM((chunks, depth, cw), b16),
            pltpu.VMEM((chunks, pairs, 2, here, cw), f32),
            pltpu.VMEM((chunks, pairs, here, cw), f32),
            pltpu.VMEM((chunks, pairs - 1, here, cw), b16),
            pltpu.VMEM((chunks, pairs - 1, here, cw), b16),
            pltpu.VMEM((pairs, 2, here, HD), f32),
            pltpu.VMEM((pairs, here, HD), f32),
            pltpu.VMEM((pairs - 1, here, HD), f32),
            pltpu.VMEM((pairs - 1, here, HD), f32),
            pltpu.VMEM((chunk_heads, here, HD), f32),
            pltpu.VMEM((chunks, inner, chunk_heads, tile, HD), b16),
            dma((chunks,)),
            dma((chunks,)), dma((chunks,)),
            dma((chunks, pairs - 1)), dma((chunks, pairs - 1)),
            dma((chunks, inner - 1)), dma((chunks, inner - 1)),
            dma, dma,
            dma((pairs - 1,)), dma((pairs - 1,)),
            dma((chunks,)),
        ],
        compiler_params=pltpu.CompilerParams(
            collective_id=0, has_side_effects=True, vmem_limit_bytes=VMEM_LIMIT
        ),
        name="project",
    )(x_first, x_second, gain, w)


def attend_kernel(
    groups, size, rows, lengths_ref, x_ref, cos_ref, sin_ref, keys_ref, values_ref, out_ref,
    in_ref, mix_ref,
):
    row = pl.program_id(0)
    tile = STEPS * rows
    per = size + 2
    slots = keys_ref.shape[1]
    scale = 1.0 / math.sqrt(HD)

    @pl.when(row == 0)
    def _():
        for k in range(groups):
            base = k * per
            turn = x_ref[base : base + size + 1].astype(jnp.float32)
            turned = turn * cos_ref[...][None] + pltpu.roll(turn, HD // 2, 2) * sin_ref[...][None]
            turned = turned.astype(jnp.bfloat16).astype(jnp.float32)
            in_ref[base * tile : (base + size + 1) * tile] = turned.reshape((size + 1) * tile, HD)
            in_ref[(base + size + 1) * tile : (base + per) * tile] = x_ref[base + size + 1].astype(
                jnp.float32
            )

    length = lengths_ref[row]
    valid = lax.broadcasted_iota(jnp.int32, (1, slots), 1) < length
    late = lax.broadcasted_iota(jnp.int32, (STEPS * size, 1), 0) >= size
    for k in range(groups):
        base = k * per * tile
        query = jnp.concatenate(
            [
                in_ref[pl.ds(base + s * rows + row, size, stride=tile), :]
                for s in range(STEPS)
            ],
            axis=0,
        )
        new_keys = [in_ref[pl.ds(base + size * tile + s * rows + row, 1), :] for s in range(STEPS)]
        new_values = [
            in_ref[pl.ds(base + (size + 1) * tile + s * rows + row, 1), :] for s in range(STEPS)
        ]
        columns = slice(k * HD, (k + 1) * HD)
        scores = (
            lax.dot_general(
                query.astype(jnp.bfloat16),
                keys_ref[0, :, columns],
                (((1,), (1,)), ((), ())),
                preferred_element_type=jnp.float32,
            )
            * scale
        )
        scores = jnp.where(valid, scores, -jnp.inf)
        extra_one = jnp.sum(query * new_keys[0], axis=1, keepdims=True) * scale
        extra_two = jnp.sum(query * new_keys[1], axis=1, keepdims=True) * scale
        extra_two = jnp.where(late, extra_two, -jnp.inf)
        top = jnp.maximum(
            jnp.max(scores, axis=1, keepdims=True), jnp.maximum(extra_one, extra_two)
        )
        weights = jnp.exp(scores - top)
        weight_one = jnp.exp(extra_one - top)
        weight_two = jnp.exp(extra_two - top)
        total = jnp.sum(weights, axis=1, keepdims=True) + weight_one + weight_two
        mixed = jnp.dot(
            weights.astype(jnp.bfloat16),
            values_ref[0, :, columns],
            preferred_element_type=jnp.float32,
        )
        mixed = (
            mixed
            + weight_one.astype(jnp.bfloat16).astype(jnp.float32) * new_values[0]
            + weight_two.astype(jnp.bfloat16).astype(jnp.float32) * new_values[1]
        )
        mixed = mixed / total
        for s in range(STEPS):
            mix_ref[pl.ds(k * size * tile + s * rows + row, size, stride=tile), :] = mixed[
                s * size : (s + 1) * size
            ]

    @pl.when(row == rows - 1)
    def _():
        out_ref[...] = mix_ref[...].reshape(out_ref.shape).astype(jnp.bfloat16)


def attend(joined, cosine, sine, keys, values, lengths):
    rows, slots, width = keys.shape
    groups = width // HD
    heads, tile, _ = joined.shape
    size = heads // groups - 2
    whole = lambda r, lens: (0, 0)
    return pl.pallas_call(
        functools.partial(attend_kernel, groups, size, rows),
        grid_spec=pltpu.PrefetchScalarGridSpec(
            num_scalar_prefetch=1,
            grid=(rows,),
            in_specs=[
                pl.BlockSpec((heads, tile, HD), lambda r, lens: (0, 0, 0)),
                pl.BlockSpec((tile, HD), whole),
                pl.BlockSpec((tile, HD), whole),
                pl.BlockSpec((1, slots, width), lambda r, lens: (r, 0, 0)),
                pl.BlockSpec((1, slots, width), lambda r, lens: (r, 0, 0)),
            ],
            out_specs=pl.BlockSpec((groups * size, tile, HD), lambda r, lens: (0, 0, 0)),
            scratch_shapes=[
                pltpu.VMEM((heads * tile, HD), jnp.float32),
                pltpu.VMEM((groups * size * tile, HD), jnp.float32),
            ],
        ),
        out_shape=jax.ShapeDtypeStruct((groups * size, tile, HD), jnp.bfloat16),
        compiler_params=pltpu.CompilerParams(vmem_limit_bytes=VMEM_LIMIT),
    )(lengths, joined, cosine, sine, keys, values)


def finish_kernel(
    dims, heads, w, out_first, out_second,
    held, flat, w_here, own, to_across, from_across, piece,
    w_sem, z_send, z_recv, keep_sem, along_send, along_recv, share_send, share_recv,
    across_send, across_recv,
):
    outer, inner, rows, chunks = dims
    gx, gy, pair, side, other, along, across = places(outer, inner)
    pairs = outer // 2
    count = heads.shape[1]
    tile = STEPS * rows
    cw = w_here.shape[2]
    depth = flat.shape[1]
    part = flat.shape[0] // inner
    groups = part // tile

    def w_copy(n):
        return pltpu.make_async_copy(w.at[:, pl.ds(n * cw, cw)], w_here.at[n], w_sem.at[n])

    for n in range(chunks):
        w_copy(n).start()
    signal_peers([other] + along + across)

    def send_z(d):
        return pltpu.make_async_remote_copy(
            src_ref=heads.at[lax.rem(gy + d + 1, inner)], dst_ref=held.at[gx, gy],
            send_sem=z_send.at[d], recv_sem=z_recv.at[d],
            device_id=across[d], device_id_type=MESH,
        )

    def source(d):
        return lax.rem(gy + inner - d, inner)

    def send_along(d, e):
        return pltpu.make_async_remote_copy(
            src_ref=held.at[gx, source(d)], dst_ref=held.at[gx, source(d)],
            send_sem=along_send.at[d, e], recv_sem=along_recv.at[d, e],
            device_id=along[e], device_id_type=MESH,
        )

    def share(d, e):
        column = 2 * lax.rem(pair + pairs - e, pairs) + side
        return pltpu.make_async_remote_copy(
            src_ref=held.at[column, source(d)], dst_ref=held.at[column, source(d)],
            send_sem=share_send.at[d, e], recv_sem=share_recv.at[d, e],
            device_id=other, device_id_type=MESH,
        )

    keep = pltpu.make_async_copy(heads.at[gy], held.at[gx, gy], keep_sem)
    keep.start()
    for d in range(inner - 1):
        send_z(d).start()
    keep.wait()
    for d in range(inner):
        if d > 0:
            send_z(d - 1).wait_recv()
        for e in range(pairs - 1):
            send_along(d, e).start()
        share(d, 0).start()
    for d in range(inner):
        for e in range(pairs - 1):
            send_along(d, e).wait_recv()
            share(d, e + 1).start()
    for d in range(inner):
        for e in range(pairs):
            share(d, e).wait_recv()

    @pl.loop(0, outer)
    def _(g):
        for h in range(count):
            flat[pl.ds(g * inner * tile, inner * tile), h * HD : (h + 1) * HD] = (
                held[g, :, h].astype(jnp.float32).reshape(inner * tile, HD).astype(jnp.bfloat16)
            )

    def send_across(n, d):
        return pltpu.make_async_remote_copy(
            src_ref=to_across.at[n, d], dst_ref=from_across.at[n, d],
            send_sem=across_send.at[n, d], recv_sem=across_recv.at[n, d],
            device_id=across[d], device_id_type=MESH,
        )

    @pl.loop(0, chunks)
    def _(n):
        w_copy(n).wait()
        own[n] = jnp.dot(flat[...], w_here[n], preferred_element_type=jnp.float32).reshape(
            inner, part, cw
        )
        for d in range(inner - 1):
            to_across[n, d] = own[n, lax.rem(gy + d + 1, inner)].astype(jnp.bfloat16)
            send_across(n, d).start()

    @pl.loop(0, chunks)
    def _(n):
        for d in range(inner - 1):
            send_across(n, d).wait()
        for j in range(cw // HD):
            columns = slice(j * HD, (j + 1) * HD)
            total = own[n, gy, :, columns]
            for d in range(inner - 1):
                total = total + from_across[n, d, :, columns].astype(jnp.float32)
            for q in range(groups):
                for s in range(STEPS):
                    piece[s, q * rows : (q + 1) * rows, :] = total[
                        q * tile + s * rows : q * tile + (s + 1) * rows
                    ]
            place = pl.ds(pl.multiple_of(n * cw + j * HD, HD), HD)
            out_first[:, place] = piece[0].astype(jnp.bfloat16)
            out_second[:, place] = piece[1].astype(jnp.bfloat16)

    for d in range(inner):
        if d > 0:
            send_z(d - 1).wait_send()
        for e in range(pairs - 1):
            send_along(d, e).wait_send()
        for e in range(pairs):
            share(d, e).wait_send()


def finish(heads, w, outer, inner, rows):
    count = heads.shape[1]
    depth, columns = w.shape
    chunks = columns // min(512, columns)
    cw = columns // chunks
    pairs = outer // 2
    tile = STEPS * rows
    total = outer * inner * tile
    part = total // inner
    dims = (outer, inner, rows, chunks)
    dma = pltpu.SemaphoreType.DMA
    vmem = pl.BlockSpec(memory_space=pltpu.VMEM)
    f32, b16 = jnp.float32, jnp.bfloat16
    shape = jax.ShapeDtypeStruct((part // STEPS, columns), b16)
    return pl.pallas_call(
        functools.partial(finish_kernel, dims),
        in_specs=[vmem, pl.BlockSpec(memory_space=pl.ANY)],
        out_specs=(vmem, vmem),
        out_shape=(shape, shape),
        scratch_shapes=[
            pltpu.VMEM((outer, inner, count, tile, HD), b16),
            pltpu.VMEM((total, depth), b16),
            pltpu.VMEM((chunks, depth, cw), b16),
            pltpu.VMEM((chunks, inner, part, cw), f32),
            pltpu.VMEM((chunks, inner - 1, part, cw), b16),
            pltpu.VMEM((chunks, inner - 1, part, cw), b16),
            pltpu.VMEM((STEPS, part // STEPS, HD), f32),
            dma((chunks,)),
            dma((inner - 1,)), dma((inner - 1,)),
            dma,
            dma((inner, pairs - 1)), dma((inner, pairs - 1)),
            dma((inner, pairs)), dma((inner, pairs)),
            dma((chunks, inner - 1)), dma((chunks, inner - 1)),
        ],
        compiler_params=pltpu.CompilerParams(
            collective_id=1, has_side_effects=True, vmem_limit_bytes=VMEM_LIMIT
        ),
        name="finish",
    )(heads, w)


def body(x_first, x_second, norm_gain, w_qkv, w_out, cache_keys, cache_values, lengths):
    outer, inner = lax.axis_size("gx"), lax.axis_size("gy")
    rows = lengths.shape[0]
    tile = STEPS * rows
    width = x_first.shape[1] * outer
    heads_here = w_qkv.shape[1] // HD

    half = HD // 2
    freq = rotary_base ** (-(jnp.arange(half, dtype=jnp.float32) * 2.0 / HD))
    position = jnp.concatenate([lengths + s for s in range(STEPS)])
    angle = position.astype(jnp.float32)[:, None] * freq
    cosine = jnp.tile(jnp.cos(angle), (1, 2))
    sine = jnp.concatenate([-jnp.sin(angle), jnp.sin(angle)], axis=1)

    joined = project(x_first, x_second, norm_gain[None], w_qkv, outer, inner, rows, width)
    joined = joined.reshape(inner * heads_here, tile, HD)
    heads = attend(joined, cosine, sine, cache_keys, cache_values, lengths)
    heads = heads.reshape(inner, heads.shape[0] // inner, tile, HD)
    return finish(heads, w_out, outer, inner, rows)


def solution(mesh):
    in_specs = (
        P(None, "gx"),
        P(None, "gx"),
        P("gx"),
        P("gx", "gy"),
        P("gy", "gx"),
        P(("gx", "gy"), None, None),
        P(("gx", "gy"), None, None),
        P(("gx", "gy")),
    )
    out_specs = (P("gy", "gx"), P("gy", "gx"))
    return jax.shard_map(body, mesh=mesh, in_specs=in_specs, out_specs=out_specs, check_vma=False)
```

```python
import functools
import math

import jax
import jax.numpy as jnp
import numpy as np
from jax import lax
from jax.experimental import pallas as pl
from jax.experimental.pallas import tpu as pltpu
from jax.sharding import PartitionSpec as P

HD = 128
norm_eps = 1e-05
rotary_base = 500000.0
STEPS = 2
BLOCK = 256
VMEM_LIMIT = 60 * 1024 * 1024
MESH = pl.DeviceIdType.MESH


def signal_peers(peers):
    barrier = pltpu.get_barrier_semaphore()
    for peer in peers:
        pl.semaphore_signal(barrier, inc=1, device_id=peer, device_id_type=MESH)
    pl.semaphore_wait(barrier, len(peers))


def remote(src, dst, send, recv, device):
    return pltpu.make_async_remote_copy(
        src_ref=src, dst_ref=dst, send_sem=send, recv_sem=recv,
        device_id=device, device_id_type=MESH,
    )


def block_kernel(
    dims, lengths, x_first, x_second, gain, freq, w_in, w_out, keys, values, result,
    x_here, k_here, v_here, weights, scaled, prod, from_other, to_along, from_along,
    sq, sq_other, sq_to, sq_along, mixed, to_across, joined,
    turned, mix, to_rows, held, flat, own, to_sum, from_sum, piece,
    x_sem, kv_sem, in_sem, out_sem, pair_send, pair_recv, along_send, along_recv,
    across_send, across_recv, sq_send, sq_recv, sqa_send, sqa_recv, own_sem,
    rows_send, rows_recv, keep_sem, gather_send, gather_recv, share_send, share_recv,
    sum_send, sum_recv,
):
    outer, inner, rows, width, groups, size, chunk_heads, chunks = dims
    gx, gy = lax.axis_index("gx"), lax.axis_index("gy")
    pairs = outer // 2
    pair, side = gx // 2, lax.rem(gx, 2)
    other = (gx + 1 - 2 * side, gy)
    along = [(2 * lax.rem(pair + d, pairs) + side, gy) for d in range(1, pairs)]
    across = [(gx, lax.rem(gy + d, inner)) for d in range(1, inner)]
    cw = chunk_heads * HD
    per_chunk = cw // BLOCK
    block = inner * rows
    here = STEPS * block
    tile = STEPS * rows
    per = size + 2
    chunks_each = chunks // groups
    slots = k_here.shape[1]
    depth = scaled.shape[1]
    out_blocks = own.shape[0]
    pieces = flat.shape[0]
    pieces_each = pieces // groups
    heads_piece = depth // HD
    part = own.shape[2]
    scale = 1.0 / math.sqrt(HD)

    x_copies = [
        pltpu.make_async_copy(x, x_here.at[s], x_sem.at[s])
        for s, x in enumerate((x_first, x_second))
    ]

    def in_copy(b):
        return pltpu.make_async_copy(
            w_in.at[:, pl.ds(pl.multiple_of(b * BLOCK, BLOCK), BLOCK)], weights.at[b], in_sem.at[b]
        )

    def out_copy(n, p):
        return pltpu.make_async_copy(
            w_out.at[
                pl.ds(p * depth, depth), pl.ds(pl.multiple_of(n * BLOCK, BLOCK), BLOCK)
            ],
            weights.at[n * pieces + p],
            out_sem.at[n, p],
        )

    kv_copies = [
        pltpu.make_async_copy(keys, k_here, kv_sem.at[0]),
        pltpu.make_async_copy(values, v_here, kv_sem.at[1]),
    ]

    def send_sq():
        return remote(sq.at[:, 1 - side], sq_other, sq_send, sq_recv, other)

    def send_sq_along(d):
        return remote(sq_to.at[d], sq_along.at[d], sqa_send.at[d], sqa_recv.at[d], along[d])

    def send_pair(n):
        return remote(
            prod.at[n, :, 1 - side], from_other.at[n], pair_send.at[n], pair_recv.at[n], other
        )

    def send_along(n, d):
        return remote(
            to_along.at[n, d], from_along.at[n, d],
            along_send.at[n, d], along_recv.at[n, d], along[d],
        )

    def columns_of(n):
        return pl.ds(n * chunk_heads, chunk_heads)

    def send_across(n, d):
        return remote(
            to_across.at[n, lax.rem(gy + d + 1, inner)], joined.at[gy, columns_of(n)],
            across_send.at[n, d], across_recv.at[n, d], across[d],
        )

    def keep_own(n):
        return pltpu.make_async_copy(
            to_across.at[n, gy], joined.at[gy, columns_of(n)], own_sem.at[n]
        )

    def source(d):
        return lax.rem(gy + inner - d, inner)

    def send_rows(j, d):
        return remote(
            to_rows.at[j, d], held.at[j, gx, gy], rows_send.at[j, d], rows_recv.at[j, d], across[d]
        )

    def keep_rows(j):
        return pltpu.make_async_copy(
            to_rows.at[j, inner - 1], held.at[j, gx, gy], keep_sem.at[j]
        )

    def gather(j, d, e):
        ref = held.at[j, gx, source(d)]
        return remote(ref, ref, gather_send.at[j, d, e], gather_recv.at[j, d, e], along[e])

    def share(j, d, e):
        ref = held.at[j, 2 * lax.rem(pair + pairs - e, pairs) + side, source(d)]
        return remote(ref, ref, share_send.at[j, d, e], share_recv.at[j, d, e], other)

    def send_sum(n, d):
        return remote(
            to_sum.at[n, d], from_sum.at[n, d], sum_send.at[n, d], sum_recv.at[n, d], across[d]
        )

    for copy in x_copies:
        copy.start()

    @pl.loop(0, chunks * per_chunk)
    def _(b):
        in_copy(b).start()

    for copy in kv_copies:
        copy.start()
    signal_peers([other] + along + across)

    wide_gain = gain[...].astype(jnp.float32).reshape(1, depth)
    for s in range(STEPS):
        x_copies[s].wait()

        @pl.loop(0, outer)
        def _(g):
            wide = x_here[s, pl.ds(pl.multiple_of(g * block, block), block), :].astype(jnp.float32)
            row = pl.multiple_of(g * here + s * block, block)
            scaled[pl.ds(row, block), :] = (wide * wide_gain).astype(jnp.bfloat16)
            total = jnp.sum(wide * wide, axis=1, keepdims=True)
            sq[g // 2, lax.rem(g, 2), s * block : (s + 1) * block, :] = jnp.broadcast_to(
                total, (block, HD)
            )

    send_sq().start()

    def pass_on(n):
        send_pair(n).wait()
        for d in range(pairs - 1):
            there = lax.rem(pair + d + 1, pairs)
            to_along[n, d] = (prod[n, there, side] + from_other[n, there]).astype(jnp.bfloat16)
            send_along(n, d).start()

    @pl.loop(0, chunks)
    def _(n):
        for c in range(per_chunk):
            b = n * per_chunk + c
            in_copy(b).wait()
            product = jnp.dot(scaled[...], weights[b], preferred_element_type=jnp.float32)
            prod[n, :, :, :, c * BLOCK : (c + 1) * BLOCK] = product.reshape(pairs, 2, here, BLOCK)
        send_pair(n).start()

        @pl.when(n == 0)
        def _():
            send_sq().wait()
            for d in range(pairs - 1):
                there = lax.rem(pair + d + 1, pairs)
                sq_to[d] = sq[there, side] + sq_other[there]
                send_sq_along(d).start()

        @pl.when(n > 0)
        def _():
            pass_on(n - 1)

    pass_on(chunks - 1)

    @pl.loop(0, out_blocks)
    def _(n):
        for p in range(pieces):
            out_copy(n, p).start()

    squares = sq[pair, side] + sq_other[pair]
    for d in range(pairs - 1):
        send_sq_along(d).wait()
        squares = squares + sq_along[d]
    sq[0, 0] = lax.rsqrt(squares / width + norm_eps)

    def settle(n):
        for d in range(pairs - 1):
            send_along(n, d).wait()
        for h in range(chunk_heads):
            columns = slice(h * HD, (h + 1) * HD)
            total = prod[n, pair, side, :, columns] + from_other[n, pair, :, columns]
            for d in range(pairs - 1):
                total = total + from_along[n, d, :, columns].astype(jnp.float32)
            total = total * sq[0, 0]
            for s in range(STEPS):
                for z in range(inner):
                    mixed[h, z * tile + s * rows : z * tile + (s + 1) * rows, :] = total[
                        s * block + z * rows : s * block + (z + 1) * rows
                    ]
            for z in range(inner):
                to_across[n, z, h] = mixed[h, z * tile : (z + 1) * tile, :].astype(jnp.bfloat16)
        for d in range(inner - 1):
            send_across(n, d).start()
        keep_own(n).start()

    @pl.loop(0, chunks_each)
    def _(n):
        settle(n)

    index = lax.broadcasted_iota(jnp.int32, (tile, HD), 0)
    lane = lax.broadcasted_iota(jnp.int32, (tile, HD), 1)
    position = jnp.zeros((tile, HD), jnp.float32)
    for s in range(STEPS):
        for i in range(rows):
            position = jnp.where(
                index == s * rows + i, (lengths[i] + s).astype(jnp.float32), position
            )
    angle = position * freq[...]
    cosine = jnp.cos(angle)
    sine = jnp.where(lane < HD // 2, -jnp.sin(angle), jnp.sin(angle))
    late = lax.broadcasted_iota(jnp.int32, (STEPS * size, 1), 0) >= size

    def forward(j, d):
        for e in range(pairs - 1):
            gather(j, d, e).start()
        share(j, d, 0).start()

    for copy in kv_copies:
        copy.wait()

    for j in range(groups):

        @pl.loop(j * chunks_each, (j + 1) * chunks_each)
        def _(n):
            keep_own(n).wait()
            for d in range(inner - 1):
                send_across(n, d).wait()

        @pl.loop(0, inner)
        def _(d):
            there = lax.rem(gy + d + 1, inner)
            turn = joined[there, j * per : j * per + size + 1].astype(jnp.float32)
            turn = turn * cosine[None] + pltpu.roll(turn, HD // 2, 2) * sine[None]
            turn = turn.astype(jnp.bfloat16).astype(jnp.float32)
            turned[: (size + 1) * tile] = turn.reshape((size + 1) * tile, HD)
            turned[(size + 1) * tile :] = joined[there, j * per + size + 1].astype(jnp.float32)
            place = pl.ds(pl.multiple_of((there * groups + j) * HD, HD), HD)
            for i in range(rows):
                valid = lax.broadcasted_iota(jnp.int32, (1, slots), 1) < lengths[i]
                query = jnp.concatenate(
                    [turned[pl.ds(s * rows + i, size, stride=tile), :] for s in range(STEPS)],
                    axis=0,
                )
                new_keys = [
                    turned[size * tile + s * rows + i : size * tile + s * rows + i + 1, :]
                    for s in range(STEPS)
                ]
                first = (size + 1) * tile
                new_values = [
                    turned[first + s * rows + i : first + s * rows + i + 1, :]
                    for s in range(STEPS)
                ]
                scores = (
                    lax.dot_general(
                        query.astype(jnp.bfloat16),
                        k_here[i, :, place],
                        (((1,), (1,)), ((), ())),
                        preferred_element_type=jnp.float32,
                    )
                    * scale
                )
                scores = jnp.where(valid, scores, -jnp.inf)
                extra_one = jnp.sum(query * new_keys[0], axis=1, keepdims=True) * scale
                extra_two = jnp.sum(query * new_keys[1], axis=1, keepdims=True) * scale
                extra_two = jnp.where(late, extra_two, -jnp.inf)
                top = jnp.maximum(
                    jnp.max(scores, axis=1, keepdims=True), jnp.maximum(extra_one, extra_two)
                )
                soft = jnp.exp(scores - top)
                soft_one = jnp.exp(extra_one - top)
                soft_two = jnp.exp(extra_two - top)
                total = jnp.sum(soft, axis=1, keepdims=True) + soft_one + soft_two
                blend = jnp.dot(
                    soft.astype(jnp.bfloat16),
                    v_here[i, :, place],
                    preferred_element_type=jnp.float32,
                )
                blend = (
                    blend
                    + soft_one.astype(jnp.bfloat16).astype(jnp.float32) * new_values[0]
                    + soft_two.astype(jnp.bfloat16).astype(jnp.float32) * new_values[1]
                )
                blend = blend / total
                for s in range(STEPS):
                    mix[pl.ds(s * rows + i, size, stride=tile), :] = blend[
                        s * size : (s + 1) * size
                    ]
            to_rows[j, d] = mix[...].reshape(size, tile, HD).astype(jnp.bfloat16)

            for c in range(inner - 1):

                @pl.when(d == c)
                def _():
                    send_rows(j, c).start()

            if j + 1 < groups:
                for c in range(chunks_each):

                    @pl.when(d == min(c, inner - 1))
                    def _():
                        settle((j + 1) * chunks_each + c)

            if j > 0:

                @pl.when(d == 0)
                def _():
                    keep_rows(j - 1).wait()
                    forward(j - 1, 0)

                for c in range(1, inner):

                    @pl.when(d == c)
                    def _():
                        send_rows(j - 1, c - 1).wait_recv()
                        forward(j - 1, c)

        keep_rows(j).start()

    last = groups - 1

    def fill(j):
        @pl.loop(0, outer)
        def _(g):
            row = pl.multiple_of(g * inner * tile, inner * tile)
            for h in range(size):
                p = j * pieces_each + h // heads_piece
                column = (h % heads_piece) * HD
                flat[p, pl.ds(row, inner * tile), column : column + HD] = (
                    held[j, g, :, h].astype(jnp.float32).reshape(inner * tile, HD)
                    .astype(jnp.bfloat16)
                )

    def share_arrived(j):
        for d in range(inner):
            for e in range(pairs - 1):
                gather(j, d, e).wait_recv()
                share(j, d, e + 1).start()

    def take_shared(j):
        for d in range(inner):
            for e in range(pairs):
                share(j, d, e).wait_recv()

    for j in range(groups - 1):
        share_arrived(j)
    keep_rows(last).wait()
    forward(last, 0)
    for d in range(1, inner):
        send_rows(last, d - 1).wait_recv()
        forward(last, d)

    for j in range(groups - 1):
        take_shared(j)
        fill(j)

        @pl.loop(0, out_blocks)
        def _(n):
            for p in range(j * pieces_each, (j + 1) * pieces_each):
                out_copy(n, p).wait()
                product = jnp.dot(
                    flat[p], weights[n * pieces + p], preferred_element_type=jnp.float32
                ).reshape(inner, part, BLOCK)
                own[n] = product if p == 0 else own[n] + product

    share_arrived(last)
    take_shared(last)
    fill(last)

    @pl.loop(0, out_blocks)
    def _(n):
        total = None if last == 0 else own[n]
        for p in range(last * pieces_each, pieces):
            out_copy(n, p).wait()
            product = jnp.dot(
                flat[p], weights[n * pieces + p], preferred_element_type=jnp.float32
            ).reshape(inner, part, BLOCK)
            total = product if total is None else total + product
        own[n] = total
        for d in range(inner - 1):
            to_sum[n, d] = own[n, lax.rem(gy + d + 1, inner)].astype(jnp.bfloat16)
            send_sum(n, d).start()

    @pl.loop(0, out_blocks)
    def _(n):
        for d in range(inner - 1):
            send_sum(n, d).wait()
        for c in range(BLOCK // HD):
            columns = slice(c * HD, (c + 1) * HD)
            total = own[n, gy, :, columns]
            for d in range(inner - 1):
                total = total + from_sum[n, d, :, columns].astype(jnp.float32)
            for q in range(part // tile):
                for s in range(STEPS):
                    piece[s, q * rows : (q + 1) * rows, :] = total[
                        q * tile + s * rows : q * tile + (s + 1) * rows
                    ]
            place = pl.ds(pl.multiple_of(n * BLOCK + c * HD, HD), HD)
            for s in range(STEPS):
                result[s, :, place] = piece[s].astype(jnp.bfloat16)

    for j in range(groups):
        for d in range(inner):
            if d > 0:
                send_rows(j, d - 1).wait_send()
            for e in range(pairs - 1):
                gather(j, d, e).wait_send()
            for e in range(pairs):
                share(j, d, e).wait_send()


def body(x_first, x_second, norm_gain, w_qkv, w_out, cache_keys, cache_values, lengths):
    outer, inner = lax.axis_size("gx"), lax.axis_size("gy")
    rows, slots, kv_width = cache_keys.shape
    depth, in_columns = w_qkv.shape
    out_depth, out_columns = w_out.shape
    width = depth * outer
    heads = in_columns // HD
    groups = kv_width // HD // inner
    size = heads // groups - 2
    chunk_heads = 6
    chunks = heads // chunk_heads
    cw = chunk_heads * HD
    pairs = outer // 2
    here = STEPS * inner * rows
    tile = STEPS * rows
    total = outer * here
    part = total // inner
    out_blocks = out_columns // BLOCK
    pieces = out_depth // depth
    dims = (outer, inner, rows, width, groups, size, chunk_heads, chunks)

    half = HD // 2
    freq = rotary_base ** (-(np.arange(half, dtype=np.float64) * 2.0 / HD))
    freq = jnp.asarray(np.tile(freq, 2)[None], jnp.float32)

    dma = pltpu.SemaphoreType.DMA
    vmem = pl.BlockSpec(memory_space=pltpu.VMEM)
    away = pl.BlockSpec(memory_space=pl.ANY)
    f32, b16 = jnp.float32, jnp.bfloat16
    result = pl.pallas_call(
        functools.partial(block_kernel, dims),
        in_specs=[
            pl.BlockSpec(memory_space=pltpu.SMEM), away, away, vmem, vmem, away, away, away, away,
        ],
        out_specs=vmem,
        out_shape=jax.ShapeDtypeStruct((STEPS, part // STEPS, out_columns), b16),
        scratch_shapes=[
            pltpu.VMEM((STEPS, outer * inner * rows, depth), b16),
            pltpu.VMEM((rows, slots, kv_width), b16),
            pltpu.VMEM((rows, slots, kv_width), b16),
            pltpu.VMEM((max(in_columns // BLOCK, out_blocks * pieces), depth, BLOCK), b16),
            pltpu.VMEM((total, depth), b16),
            pltpu.VMEM((chunks, pairs, 2, here, cw), f32),
            pltpu.VMEM((chunks, pairs, here, cw), f32),
            pltpu.VMEM((chunks, pairs - 1, here, cw), b16),
            pltpu.VMEM((chunks, pairs - 1, here, cw), b16),
            pltpu.VMEM((pairs, 2, here, HD), f32),
            pltpu.VMEM((pairs, here, HD), f32),
            pltpu.VMEM((pairs - 1, here, HD), f32),
            pltpu.VMEM((pairs - 1, here, HD), f32),
            pltpu.VMEM((chunk_heads, here, HD), f32),
            pltpu.VMEM((chunks, inner, chunk_heads, tile, HD), b16),
            pltpu.VMEM((inner, heads, tile, HD), b16),
            pltpu.VMEM(((size + 2) * tile, HD), f32),
            pltpu.VMEM((size * tile, HD), f32),
            pltpu.VMEM((groups, inner, size, tile, HD), b16),
            pltpu.VMEM((groups, outer, inner, size, tile, HD), b16),
            pltpu.VMEM((pieces, total, depth), b16),
            pltpu.VMEM((out_blocks, inner, part, BLOCK), f32),
            pltpu.VMEM((out_blocks, inner - 1, part, BLOCK), b16),
            pltpu.VMEM((out_blocks, inner - 1, part, BLOCK), b16),
            pltpu.VMEM((STEPS, part // STEPS, HD), f32),
            dma((STEPS,)), dma((2,)), dma((in_columns // BLOCK,)), dma((out_blocks, pieces)),
            dma((chunks,)), dma((chunks,)),
            dma((chunks, pairs - 1)), dma((chunks, pairs - 1)),
            dma((chunks, inner - 1)), dma((chunks, inner - 1)),
            dma, dma, dma((pairs - 1,)), dma((pairs - 1,)), dma((chunks,)),
            dma((groups, inner - 1)), dma((groups, inner - 1)), dma((groups,)),
            dma((groups, inner, pairs - 1)), dma((groups, inner, pairs - 1)),
            dma((groups, inner, pairs)), dma((groups, inner, pairs)),
            dma((out_blocks, inner - 1)), dma((out_blocks, inner - 1)),
        ],
        compiler_params=pltpu.CompilerParams(
            collective_id=0, has_side_effects=True, vmem_limit_bytes=VMEM_LIMIT
        ),
        name="decode_block",
    )(lengths, x_first, x_second, norm_gain, freq, w_qkv, w_out, cache_keys, cache_values)
    return result[0], result[1]


def solution(mesh):
    in_specs = (
        P(None, "gx"),
        P(None, "gx"),
        P("gx"),
        P("gx", "gy"),
        P("gy", "gx"),
        P(("gx", "gy"), None, None),
        P(("gx", "gy"), None, None),
        P(("gx", "gy")),
    )
    out_specs = (P("gy", "gx"), P("gy", "gx"))
    return jax.shard_map(body, mesh=mesh, in_specs=in_specs, out_specs=out_specs, check_vma=False)
```

```python
import functools
import math

import jax
import jax.numpy as jnp
import numpy as np
from jax import lax
from jax.experimental import pallas as pl
from jax.experimental.pallas import tpu as pltpu
from jax.sharding import PartitionSpec as P

HD = 128
norm_eps = 1e-05
rotary_base = 500000.0
STEPS = 2
HALVES = 2
SUB = 8
EXTRA = 16
VMEM_LIMIT = 62 * 1024 * 1024
MESH = pl.DeviceIdType.MESH


def remote(src, dst, send, recv, device):
    return pltpu.make_async_remote_copy(
        src_ref=src, dst_ref=dst, send_sem=send, recv_sem=recv,
        device_id=device, device_id_type=MESH,
    )


def block_kernel(
    dims, lengths, x_first, x_second, gain, freq, w_in, w_out, keys, values, result,
    x_here, k_here, v_here, weights, scaled, prod, from_other, to_along, from_along,
    sq, sq_other, sq_to, sq_along, mixed, to_across, joined,
    turned, spread, fresh, mix, to_rows, held, parted, flat, own, to_sum, from_sum, piece,
    x_sem, kv_sem, in_sem, out_sem, pair_send, pair_recv, along_send, along_recv,
    across_send, across_recv, sq_send, sq_recv, sqa_send, sqa_recv, own_sem,
    rows_send, rows_recv, keep_sem, gather_send, gather_recv, share_send, share_recv,
    sum_send, sum_recv,
):
    outer, inner, rows, width, groups, size, chunk_heads, chunks = dims
    gx, gy = lax.axis_index("gx"), lax.axis_index("gy")
    pairs = outer // 2
    pair, side = gx // 2, lax.rem(gx, 2)
    other = (gx + 1 - 2 * side, gy)
    along = [(2 * lax.rem(pair + d, pairs) + side, gy) for d in range(1, pairs)]
    across = [(gx, lax.rem(gy + d, inner)) for d in range(1, inner)]
    cw = chunk_heads * HD
    block = inner * rows
    here = STEPS * block
    half_rows = rows // HALVES
    tile = STEPS * half_rows
    per_tile = SUB // tile
    per = size + 2
    slots = k_here.shape[1] - EXTRA
    half = here // HALVES
    depth = scaled.shape[1]
    out_blocks = own.shape[1]
    pieces = flat.shape[1]
    part = own.shape[3]
    scale = 1.0 / math.sqrt(HD)

    x_copies = [
        pltpu.make_async_copy(x, x_here.at[s], x_sem.at[s])
        for s, x in enumerate((x_first, x_second))
    ]

    def in_copy(b):
        return pltpu.make_async_copy(
            w_in.at[:, pl.ds(pl.multiple_of(b * cw, cw), cw)], weights.at[b], in_sem.at[b]
        )

    def out_copy(n, p):
        return pltpu.make_async_copy(
            w_out.at[
                pl.ds(p * depth, depth), pl.ds(pl.multiple_of(n * cw, cw), cw)
            ],
            weights.at[n * pieces + p],
            out_sem.at[n, p],
        )

    kv_copies = [
        pltpu.make_async_copy(keys, k_here.at[:, pl.ds(0, slots)], kv_sem.at[0]),
        pltpu.make_async_copy(values, v_here.at[:, pl.ds(0, slots)], kv_sem.at[1]),
    ]

    def send_sq():
        return remote(sq.at[:, 1 - side], sq_other, sq_send, sq_recv, other)

    def send_sq_along(d):
        return remote(sq_to.at[d], sq_along.at[d], sqa_send.at[d], sqa_recv.at[d], along[d])

    def send_pair(n):
        return remote(
            prod.at[n, :, 1 - side], from_other.at[n], pair_send.at[n], pair_recv.at[n], other
        )

    def send_along(n, f, d):
        return remote(
            to_along.at[n, f, d], from_along.at[n, f, d],
            along_send.at[n, f, d], along_recv.at[n, f, d], along[d],
        )

    def send_across(n, f, d):
        return remote(
            to_across.at[n, f, lax.rem(gy + d + 1, inner)], joined.at[gy, n, f],
            across_send.at[n, f, d], across_recv.at[n, f, d], across[d],
        )

    def keep_own(n, f):
        return pltpu.make_async_copy(
            to_across.at[n, f, gy], joined.at[gy, n, f], own_sem.at[n, f]
        )

    def source(d):
        return lax.rem(gy + inner - d, inner)

    def send_rows(f, d):
        return remote(
            to_rows.at[f, d], held.at[f, gx, gy], rows_send.at[f, d], rows_recv.at[f, d], across[d]
        )

    def keep_rows(f):
        return pltpu.make_async_copy(
            to_rows.at[f, inner - 1], held.at[f, gx, gy], keep_sem.at[f]
        )

    def gather(f, d, e):
        ref = held.at[f, gx, source(d)]
        return remote(ref, ref, gather_send.at[f, d, e], gather_recv.at[f, d, e], along[e])

    def share(f, d, e):
        ref = held.at[f, 2 * lax.rem(pair + pairs - e, pairs) + side, source(d)]
        return remote(ref, ref, share_send.at[f, d, e], share_recv.at[f, d, e], other)

    def send_sum(f, n, d):
        return remote(
            to_sum.at[f, n, d], from_sum.at[f, n, d],
            sum_send.at[f, n, d], sum_recv.at[f, n, d], across[d],
        )

    for copy in x_copies:
        copy.start()

    @pl.loop(0, chunks)
    def _(b):
        in_copy(b).start()

    for copy in kv_copies:
        copy.start()

    barrier = pltpu.get_barrier_semaphore()
    peers = [other] + along + across
    for peer in peers:
        pl.semaphore_signal(barrier, inc=1, device_id=peer, device_id_type=MESH)

    to = lax.broadcasted_iota(jnp.int32, (here, here), 0)
    step = lax.rem(lax.div(to, half_rows), STEPS)
    member = lax.rem(lax.div(to, tile), inner)
    start = lax.div(to, half) * half_rows + lax.rem(to, half_rows)
    source_row = step * block + member * rows + start
    order = jnp.where(
        source_row == lax.broadcasted_iota(jnp.int32, (here, here), 1), 1.0, 0.0
    ).astype(jnp.bfloat16)
    wide_gain = gain[...].astype(jnp.float32).reshape(1, depth)
    for copy in x_copies:
        copy.wait()

    @pl.loop(0, outer)
    def _(g):
        parts = []
        for s in range(STEPS):
            wide = x_here[s, pl.ds(pl.multiple_of(g * block, block), block), :].astype(jnp.float32)
            parts.append((wide * wide_gain).astype(jnp.bfloat16))
            total = jnp.sum(wide * wide, axis=1, keepdims=True)
            sq[g // 2, lax.rem(g, 2), s * block : (s + 1) * block, :] = jnp.broadcast_to(
                total, (block, HD)
            )
        scaled[pl.ds(pl.multiple_of(g * here, here), here), :] = jnp.dot(
            order, jnp.concatenate(parts, axis=0), preferred_element_type=jnp.float32
        ).astype(jnp.bfloat16)

    pl.semaphore_wait(barrier, len(peers))
    send_sq().start()

    def pass_on(n):
        send_pair(n).wait()
        for d in range(pairs - 1):
            there = lax.rem(pair + d + 1, pairs)
            both = (prod[n, there, side] + from_other[n, there]).astype(jnp.bfloat16)
            for f in range(HALVES):
                to_along[n, f, d] = both[f * half : (f + 1) * half]
            send_along(n, 0, d).start()

    @pl.loop(0, chunks)
    def _(n):
        in_copy(n).wait()
        product = jnp.dot(scaled[...], weights[n], preferred_element_type=jnp.float32)
        prod[n] = product.reshape(pairs, 2, here, cw)
        send_pair(n).start()

        @pl.when(n == 0)
        def _():
            send_sq().wait()
            for d in range(pairs - 1):
                there = lax.rem(pair + d + 1, pairs)
                sq_to[d] = sq[there, side] + sq_other[there]
                send_sq_along(d).start()

        @pl.when(n > 0)
        def _():
            pass_on(n - 1)

    pass_on(chunks - 1)

    @pl.loop(0, chunks)
    def _(n):
        for f in range(1, HALVES):
            for d in range(pairs - 1):
                send_along(n, f, d).start()

    @pl.loop(0, out_blocks)
    def _(n):
        for p in range(pieces):
            out_copy(n, p).start()

    squares = sq[pair, side] + sq_other[pair]
    for d in range(pairs - 1):
        send_sq_along(d).wait()
        squares = squares + sq_along[d]
    factor = lax.rsqrt(squares / width + norm_eps)
    for f in range(HALVES):
        for z in range(inner):
            for s in range(STEPS):
                target = f * half + z * tile + s * half_rows
                row = s * block + z * rows + f * half_rows
                sq[0, 0, target : target + half_rows, :] = factor[row : row + half_rows]

    index = lax.rem(lax.broadcasted_iota(jnp.int32, (SUB, HD), 0), tile)
    lane = lax.broadcasted_iota(jnp.int32, (SUB, HD), 1)
    cosines, sines = [], []
    for f in range(HALVES):
        position = jnp.zeros((SUB, HD), jnp.float32)
        for s in range(STEPS):
            for i in range(half_rows):
                position = jnp.where(
                    index == s * half_rows + i,
                    (lengths[f * half_rows + i] + s).astype(jnp.float32),
                    position,
                )
        angle = position * freq[...]
        cosines.append(jnp.cos(angle))
        sines.append(jnp.where(lane < HD // 2, -jnp.sin(angle), jnp.sin(angle)))

    def settle(n, f):
        for d in range(pairs - 1):
            send_along(n, f, d).wait()
        span = slice(f * half, (f + 1) * half)
        for h in range(chunk_heads):
            columns = slice(h * HD, (h + 1) * HD)
            total = prod[n, pair, side, span, columns] + from_other[n, pair, span, columns]
            for d in range(pairs - 1):
                total = total + from_along[n, f, d, :, columns].astype(jnp.float32)
            total = total * sq[0, 0, span, :]
            for z in range(inner):
                mixed[z, h * tile : (h + 1) * tile, :] = total[z * tile : (z + 1) * tile]
        for z in range(inner):
            to_across[n, f, z] = (
                mixed[z].reshape(chunk_heads // per_tile, SUB, HD).astype(jnp.bfloat16)
            )
        for d in range(inner - 1):
            send_across(n, f, d).start()
        keep_own(n, f).start()

    early = chunks // 2

    @pl.loop(0, chunks)
    def _(n):
        settle(n, 0)

    @pl.loop(0, early)
    def _(n):
        settle(n, 1)

    upper = lax.broadcasted_iota(jnp.int32, (SUB, HD), 0) < tile
    queries = size // per_tile
    kv_heads = inner * groups
    columns = kv_heads * STEPS * size
    slot = lax.broadcasted_iota(jnp.int32, (slots + EXTRA, columns), 0)
    column = lax.broadcasted_iota(jnp.int32, (1, columns), 1)
    newest = jnp.where(lax.rem(column, STEPS * size) >= size, slots + 1, slots)

    def forward(f, d):
        for e in range(pairs - 1):
            gather(f, d, e).start()
        share(f, d, 0).start()

    def forward_all(f):
        keep_rows(f).wait()
        forward(f, 0)
        for d in range(1, inner):
            send_rows(f, d - 1).wait_recv()
            forward(f, d)

    fresh[...] = jnp.zeros_like(fresh)

    @pl.loop(0, half_rows)
    def _(i):
        spread[i] = jnp.zeros(spread.shape[1:], jnp.bfloat16)

    for copy in kv_copies:
        copy.wait()

    for f in range(HALVES):

        @pl.loop(0, chunks)
        def _(n):
            if f > 0:

                @pl.when(n >= early)
                def _():
                    settle(n, f)

        @pl.loop(0, chunks)
        def _(n):
            keep_own(n, f).wait()
            for d in range(inner - 1):
                send_across(n, f, d).wait()

        if f > 0:
            forward_all(f - 1)

        @pl.loop(0, inner)
        def _(y):
            here_now = joined[y, :, f].reshape(groups * per * tile // SUB, SUB, HD)
            for j in range(groups):
                k = y * groups + j
                turn = here_now[j * per * tile // SUB : (j + 1) * per * tile // SUB]
                turn = turn.astype(jnp.float32)
                turned_now = turn * cosines[f][None] + pltpu.roll(turn, HD // 2, 2) * sines[f][None]
                turned_now = turned_now.astype(jnp.bfloat16).astype(jnp.float32)
                turned[j, : size * tile] = turned_now[:queries].reshape(size * tile, HD)
                turned[j, size * tile :] = jnp.where(upper, turned_now[queries], turn[queries])
                place = pl.ds(pl.multiple_of(k * HD, HD), HD)
                band = pl.ds(pl.multiple_of(k * STEPS * size, STEPS * size), STEPS * size)
                for i in range(half_rows):
                    query = jnp.concatenate(
                        [
                            turned[j, pl.ds(s * half_rows + i, size, stride=tile), :]
                            for s in range(STEPS)
                        ],
                        axis=0,
                    )
                    spread[i, band, place] = query.astype(jnp.bfloat16)
                    for s in range(STEPS):
                        for c in range(2):
                            row = (size + c) * tile + s * half_rows + i
                            fresh[i, c, s : s + 1, place] = turned[j, row : row + 1, :]

        for i in range(half_rows):
            row = f * half_rows + i
            k_here[row, slots:, :] = fresh[i, 0].astype(jnp.bfloat16)
            v_here[row, slots:, :] = fresh[i, 1].astype(jnp.bfloat16)
            scores = (
                lax.dot_general(
                    k_here[row],
                    spread[i],
                    (((1,), (1,)), ((), ())),
                    preferred_element_type=jnp.float32,
                )
                * scale
            )
            valid = (slot < lengths[row]) | ((slot >= slots) & (slot <= newest))
            scores = jnp.where(valid, scores, -jnp.inf)
            soft = jnp.exp(scores - jnp.max(scores, axis=0, keepdims=True))
            total = jnp.sum(soft, axis=0, keepdims=True)
            total = jnp.broadcast_to(total, (SUB, columns)).T
            soft = soft.astype(jnp.bfloat16).T
            for k in range(kv_heads):
                band = slice(k * STEPS * size, (k + 1) * STEPS * size)
                blend = jnp.dot(
                    soft[band],
                    v_here[row, :, k * HD : (k + 1) * HD],
                    preferred_element_type=jnp.float32,
                )
                blend = blend / total[band, 0:1]
                for s in range(STEPS):
                    mix[k, pl.ds(s * half_rows + i, size, stride=tile), :] = blend[
                        s * size : (s + 1) * size
                    ]

        for d in range(inner):
            there = lax.rem(gy + d + 1, inner)
            for j in range(groups):
                to_rows[f, d, j] = (
                    mix[there * groups + j].reshape(queries, SUB, HD).astype(jnp.bfloat16)
                )
            if d < inner - 1:
                send_rows(f, d).start()
        keep_rows(f).start()

    heads_piece = depth // HD
    span = inner * tile

    def pass_side(f):
        for d in range(inner):
            for e in range(pairs - 1):
                gather(f, d, e).wait_recv()
                share(f, d, e + 1).start()

    def bring(f):
        for d in range(inner):
            for e in range(pairs):
                share(f, d, e).wait_recv()

        @pl.loop(0, outer)
        def _(g):
            place = pl.ds(pl.multiple_of(g * span, span), span)
            for j in range(groups):
                for q in range(queries):
                    both = held[f, g, :, j, q].astype(jnp.float32)
                    for t in range(per_tile):
                        for z in range(inner):
                            parted[q, t, z * tile : (z + 1) * tile, :] = both[
                                z, t * tile : (t + 1) * tile
                            ]
                    for t in range(per_tile):
                        head = j * size + q * per_tile + t
                        column = (head % heads_piece) * HD
                        flat[f, head // heads_piece, place, column : column + HD] = parted[
                            q, t
                        ].astype(jnp.bfloat16)

    for f in range(HALVES):
        if f < HALVES - 1:
            pass_side(f)
        if f == max(HALVES - 2, 0):
            forward_all(HALVES - 1)
        if f == HALVES - 1:
            pass_side(f)
        bring(f)

        @pl.loop(0, out_blocks)
        def _(n):
            total = None
            for p in range(pieces):
                if f == 0:
                    out_copy(n, p).wait()
                product = jnp.dot(
                    flat[f, p], weights[n * pieces + p], preferred_element_type=jnp.float32
                )
                total = product if total is None else total + product
            own[f, n] = total.reshape(inner, part, cw)
            for d in range(inner - 1):
                to_sum[f, n, d] = own[f, n, lax.rem(gy + d + 1, inner)].astype(jnp.bfloat16)
                send_sum(f, n, d).start()

    for f in range(HALVES):

        @pl.loop(0, out_blocks)
        def _(n):
            for d in range(inner - 1):
                send_sum(f, n, d).wait()
            for c in range(cw // HD):
                columns = slice(c * HD, (c + 1) * HD)
                total = own[f, n, gy, :, columns]
                for d in range(inner - 1):
                    total = total + from_sum[f, n, d, :, columns].astype(jnp.float32)
                for q in range(part // tile):
                    for s in range(STEPS):
                        start = q * tile + s * half_rows
                        target = q * rows + f * half_rows
                        place = pl.ds(pl.multiple_of(n * cw + c * HD, HD), HD)
                        piece[s, target : target + half_rows, place] = total[
                            start : start + half_rows
                        ]

    for s in range(STEPS):
        result[s] = piece[s].astype(jnp.bfloat16)

    for f in range(HALVES):
        for d in range(inner):
            if d > 0:
                send_rows(f, d - 1).wait_send()
            for e in range(pairs - 1):
                gather(f, d, e).wait_send()
            for e in range(pairs):
                share(f, d, e).wait_send()


def body(x_first, x_second, norm_gain, w_qkv, w_out, cache_keys, cache_values, lengths):
    outer, inner = lax.axis_size("gx"), lax.axis_size("gy")
    rows, slots, kv_width = cache_keys.shape
    depth, in_columns = w_qkv.shape
    out_depth, out_columns = w_out.shape
    width = depth * outer
    heads = in_columns // HD
    groups = kv_width // HD // inner
    size = heads // groups - 2
    chunk_heads = 4 if in_columns % (4 * HD) == 0 and out_columns % (4 * HD) == 0 else 2
    chunks = heads // chunk_heads
    cw = chunk_heads * HD
    pairs = outer // 2
    here = STEPS * inner * rows
    tile = STEPS * rows // HALVES
    queries = size * tile // SUB
    total = outer * here // HALVES
    part = total // inner
    out_blocks = out_columns // cw
    pieces = out_depth // depth
    dims = (outer, inner, rows, width, groups, size, chunk_heads, chunks)

    half = HD // 2
    freq = rotary_base ** (-(np.arange(half, dtype=np.float64) * 2.0 / HD))
    freq = jnp.asarray(np.tile(freq, 2)[None], jnp.float32)

    dma = pltpu.SemaphoreType.DMA
    vmem = pl.BlockSpec(memory_space=pltpu.VMEM)
    away = pl.BlockSpec(memory_space=pl.ANY)
    f32, b16 = jnp.float32, jnp.bfloat16
    result = pl.pallas_call(
        functools.partial(block_kernel, dims),
        in_specs=[
            pl.BlockSpec(memory_space=pltpu.SMEM), away, away, vmem, vmem, away, away, away, away,
        ],
        out_specs=vmem,
        out_shape=jax.ShapeDtypeStruct((STEPS, HALVES * part // STEPS, out_columns), b16),
        scratch_shapes=[
            pltpu.VMEM((STEPS, outer * inner * rows, depth), b16),
            pltpu.VMEM((rows, slots + EXTRA, kv_width), b16),
            pltpu.VMEM((rows, slots + EXTRA, kv_width), b16),
            pltpu.VMEM((max(in_columns // cw, out_blocks * pieces), depth, cw), b16),
            pltpu.VMEM((outer * here, depth), b16),
            pltpu.VMEM((chunks, pairs, 2, here, cw), f32),
            pltpu.VMEM((chunks, pairs, here, cw), f32),
            pltpu.VMEM((chunks, HALVES, pairs - 1, here // HALVES, cw), b16),
            pltpu.VMEM((chunks, HALVES, pairs - 1, here // HALVES, cw), b16),
            pltpu.VMEM((pairs, 2, here, HD), f32),
            pltpu.VMEM((pairs, here, HD), f32),
            pltpu.VMEM((pairs - 1, here, HD), f32),
            pltpu.VMEM((pairs - 1, here, HD), f32),
            pltpu.VMEM((inner, chunk_heads * tile, HD), f32),
            pltpu.VMEM((chunks, HALVES, inner, chunk_heads * tile // SUB, SUB, HD), b16),
            pltpu.VMEM((inner, chunks, HALVES, chunk_heads * tile // SUB, SUB, HD), b16),
            pltpu.VMEM((groups, (size + 2) * tile, HD), f32),
            pltpu.VMEM((rows // HALVES, kv_width // HD * STEPS * size, kv_width), b16),
            pltpu.VMEM((rows // HALVES, 2, EXTRA, kv_width), f32),
            pltpu.VMEM((kv_width // HD, size * tile, HD), f32),
            pltpu.VMEM((HALVES, inner, groups, queries, SUB, HD), b16),
            pltpu.VMEM((HALVES, outer, inner, groups, queries, SUB, HD), b16),
            pltpu.VMEM((queries, SUB // tile, inner * tile, HD), f32),
            pltpu.VMEM((HALVES, pieces, total, depth), b16),
            pltpu.VMEM((HALVES, out_blocks, inner, part, cw), f32),
            pltpu.VMEM((HALVES, out_blocks, inner - 1, part, cw), b16),
            pltpu.VMEM((HALVES, out_blocks, inner - 1, part, cw), b16),
            pltpu.VMEM((STEPS, HALVES * part // STEPS, out_columns), f32),
            dma((STEPS,)), dma((2,)), dma((in_columns // cw,)), dma((out_blocks, pieces)),
            dma((chunks,)), dma((chunks,)),
            dma((chunks, HALVES, pairs - 1)), dma((chunks, HALVES, pairs - 1)),
            dma((chunks, HALVES, inner - 1)), dma((chunks, HALVES, inner - 1)),
            dma, dma, dma((pairs - 1,)), dma((pairs - 1,)), dma((chunks, HALVES)),
            dma((HALVES, inner - 1)), dma((HALVES, inner - 1)), dma((HALVES,)),
            dma((HALVES, inner, pairs - 1)), dma((HALVES, inner, pairs - 1)),
            dma((HALVES, inner, pairs)), dma((HALVES, inner, pairs)),
            dma((HALVES, out_blocks, inner - 1)), dma((HALVES, out_blocks, inner - 1)),
        ],
        compiler_params=pltpu.CompilerParams(
            collective_id=0, has_side_effects=True, vmem_limit_bytes=VMEM_LIMIT
        ),
        name="decode_block",
    )(lengths, x_first, x_second, norm_gain, freq, w_qkv, w_out, cache_keys, cache_values)
    return result[0], result[1]


def solution(mesh):
    in_specs = (
        P(None, "gx"),
        P(None, "gx"),
        P("gx"),
        P("gx", "gy"),
        P("gy", "gx"),
        P(("gx", "gy"), None, None),
        P(("gx", "gy"), None, None),
        P(("gx", "gy")),
    )
    out_specs = (P("gy", "gx"), P("gy", "gx"))
    return jax.shard_map(body, mesh=mesh, in_specs=in_specs, out_specs=out_specs, check_vma=False)
```

```python
import functools
import math

import jax
import jax.numpy as jnp
import numpy as np
from jax import lax
from jax.experimental import pallas as pl
from jax.experimental.pallas import tpu as pltpu
from jax.sharding import PartitionSpec as P

HD = 128
norm_eps = 1e-05
rotary_base = 500000.0
STEPS = 2
HALVES = 2
SUB = 8
EXTRA = 16
VMEM_LIMIT = 62 * 1024 * 1024
MESH = pl.DeviceIdType.MESH


def remote(src, dst, send, recv, device):
    return pltpu.make_async_remote_copy(
        src_ref=src, dst_ref=dst, send_sem=send, recv_sem=recv,
        device_id=device, device_id_type=MESH,
    )


def block_kernel(
    dims, lengths, x_first, x_second, gain, freq, w_in, w_out, keys, values, result,
    x_here, k_here, v_here, weights, scaled, prod, from_other, to_along, from_along,
    sq, sq_other, sq_to, sq_along, mixed, to_across, joined,
    turned, spread, fresh, mix, to_rows, held, parted, flat, own, to_sum, from_sum, piece,
    x_sem, kv_sem, in_sem, out_sem, pair_send, pair_recv, along_send, along_recv,
    across_send, across_recv, sq_send, sq_recv, sqa_send, sqa_recv, own_sem,
    rows_send, rows_recv, keep_sem, gather_send, gather_recv, share_send, share_recv,
    sum_send, sum_recv,
):
    outer, inner, rows, width, groups, size, chunk_heads, chunks = dims
    gx, gy = lax.axis_index("gx"), lax.axis_index("gy")
    pairs = outer // 2
    pair, side = gx // 2, lax.rem(gx, 2)
    other = (gx + 1 - 2 * side, gy)
    along = [(2 * lax.rem(pair + d, pairs) + side, gy) for d in range(1, pairs)]
    across = [(gx, lax.rem(gy + d, inner)) for d in range(1, inner)]
    cw = chunk_heads * HD
    block = inner * rows
    here = STEPS * block
    half_rows = rows // HALVES
    tile = STEPS * half_rows
    per_tile = SUB // tile
    per = size + 2
    slots = k_here.shape[1] - EXTRA
    half = here // HALVES
    depth = scaled.shape[1]
    out_blocks = own.shape[1]
    pieces = flat.shape[1]
    part = own.shape[3]
    scale = 1.0 / math.sqrt(HD)

    x_copies = [
        pltpu.make_async_copy(x, x_here.at[s], x_sem.at[s])
        for s, x in enumerate((x_first, x_second))
    ]

    def in_copy(b):
        return pltpu.make_async_copy(
            w_in.at[:, pl.ds(pl.multiple_of(b * cw, cw), cw)], weights.at[b], in_sem.at[b]
        )

    def out_copy(n, p):
        return pltpu.make_async_copy(
            w_out.at[
                pl.ds(p * depth, depth), pl.ds(pl.multiple_of(n * cw, cw), cw)
            ],
            weights.at[n * pieces + p],
            out_sem.at[n],
        )

    def out_ready(n):
        ref = weights.at[pl.ds(n * pieces, pieces)]
        return pltpu.make_async_copy(ref, ref, out_sem.at[n])

    kv_copies = [
        pltpu.make_async_copy(keys, k_here.at[:, pl.ds(0, slots)], kv_sem.at[0]),
        pltpu.make_async_copy(values, v_here.at[:, pl.ds(0, slots)], kv_sem.at[1]),
    ]

    def send_sq():
        return remote(sq.at[:, 1 - side], sq_other, sq_send, sq_recv, other)

    def send_sq_along(d):
        return remote(sq_to.at[d], sq_along.at[d], sqa_send, sqa_recv, along[d])

    def send_pair(n):
        return remote(
            prod.at[n, :, 1 - side], from_other.at[n], pair_send, pair_recv.at[n], other
        )

    def send_along(n, f, d):
        return remote(
            to_along.at[n, f, d], from_along.at[n, f, d],
            along_send.at[f], along_recv.at[n, f], along[d],
        )

    def send_across(n, f, d):
        return remote(
            to_across.at[n, f, lax.rem(gy + d + 1, inner)], joined.at[gy, n, f],
            across_send.at[f], across_recv.at[f], across[d],
        )

    def keep_own(n, f):
        return pltpu.make_async_copy(
            to_across.at[n, f, gy], joined.at[gy, n, f], own_sem.at[f]
        )

    def source(d):
        return lax.rem(gy + inner - d, inner)

    def send_rows(f, d):
        return remote(
            to_rows.at[f, d], held.at[f, gx, gy], rows_send.at[f], rows_recv.at[f, d], across[d]
        )

    def keep_rows(f):
        return pltpu.make_async_copy(
            to_rows.at[f, inner - 1], held.at[f, gx, gy], keep_sem.at[f]
        )

    def gather(f, d, e):
        ref = held.at[f, gx, source(d)]
        return remote(ref, ref, gather_send.at[f], gather_recv.at[f, e], along[e])

    def share(f, e):
        ref = held.at[f, 2 * lax.rem(pair + pairs - e, pairs) + side]
        return remote(ref, ref, share_send.at[f], share_recv.at[f, e], other)

    def send_sum(f, n, d):
        return remote(
            to_sum.at[f, n, d], from_sum.at[f, n, d],
            sum_send.at[f], sum_recv.at[f, n], across[d],
        )

    def arrived(ref, sem):
        pltpu.make_async_copy(ref, ref, sem).wait()

    for copy in x_copies:
        copy.start()

    @pl.loop(0, chunks)
    def _(b):
        in_copy(b).start()

    for copy in kv_copies:
        copy.start()

    barrier = pltpu.get_barrier_semaphore()
    peers = [other] + along + across
    for peer in peers:
        pl.semaphore_signal(barrier, inc=1, device_id=peer, device_id_type=MESH)

    to = lax.broadcasted_iota(jnp.int32, (here, here), 0)
    step = lax.rem(lax.div(to, half_rows), STEPS)
    member = lax.rem(lax.div(to, tile), inner)
    start = lax.div(to, half) * half_rows + lax.rem(to, half_rows)
    source_row = step * block + member * rows + start
    order = jnp.where(
        source_row == lax.broadcasted_iota(jnp.int32, (here, here), 1), 1.0, 0.0
    ).astype(jnp.bfloat16)
    wide_gain = gain[...].astype(jnp.float32).reshape(1, depth)
    for copy in x_copies:
        copy.wait()

    @pl.loop(0, outer)
    def _(g):
        parts = []
        for s in range(STEPS):
            wide = x_here[s, pl.ds(pl.multiple_of(g * block, block), block), :].astype(jnp.float32)
            parts.append((wide * wide_gain).astype(jnp.bfloat16))
            total = jnp.sum(wide * wide, axis=1, keepdims=True)
            sq[g // 2, lax.rem(g, 2), s * block : (s + 1) * block, :] = jnp.broadcast_to(
                total, (block, HD)
            )
        scaled[pl.ds(pl.multiple_of(g * here, here), here), :] = jnp.dot(
            order, jnp.concatenate(parts, axis=0), preferred_element_type=jnp.float32
        ).astype(jnp.bfloat16)

    pl.semaphore_wait(barrier, len(peers))
    send_sq().start()

    def pass_on(n):
        send_pair(n).wait_recv()
        for d in range(pairs - 1):
            there = lax.rem(pair + d + 1, pairs)
            both = (prod[n, there, side] + from_other[n, there]).astype(jnp.bfloat16)
            for f in range(HALVES):
                to_along[n, f, d] = both[f * half : (f + 1) * half]
            send_along(n, 0, d).start()

    @pl.loop(0, chunks)
    def _(n):
        in_copy(n).wait()
        product = jnp.dot(scaled[...], weights[n], preferred_element_type=jnp.float32)
        prod[n] = product.reshape(pairs, 2, here, cw)
        send_pair(n).start()

        @pl.when(n == 0)
        def _():
            send_sq().wait()
            for d in range(pairs - 1):
                there = lax.rem(pair + d + 1, pairs)
                sq_to[d] = sq[there, side] + sq_other[there]
                send_sq_along(d).start()

        @pl.when(n > 0)
        def _():
            pass_on(n - 1)

    pass_on(chunks - 1)

    @pl.loop(0, chunks)
    def _(n):
        for f in range(1, HALVES):
            for d in range(pairs - 1):
                send_along(n, f, d).start()

    @pl.loop(0, out_blocks)
    def _(n):
        for p in range(pieces):
            out_copy(n, p).start()

    squares = sq[pair, side] + sq_other[pair]
    arrived(sq_along, sqa_recv)
    for d in range(pairs - 1):
        squares = squares + sq_along[d]
    factor = lax.rsqrt(squares / width + norm_eps)
    for f in range(HALVES):
        for z in range(inner):
            for s in range(STEPS):
                target = f * half + z * tile + s * half_rows
                row = s * block + z * rows + f * half_rows
                sq[0, 0, target : target + half_rows, :] = factor[row : row + half_rows]

    index = lax.rem(lax.broadcasted_iota(jnp.int32, (SUB, HD), 0), tile)
    lane = lax.broadcasted_iota(jnp.int32, (SUB, HD), 1)
    cosines, sines = [], []
    for f in range(HALVES):
        position = jnp.zeros((SUB, HD), jnp.float32)
        for s in range(STEPS):
            for i in range(half_rows):
                position = jnp.where(
                    index == s * half_rows + i,
                    (lengths[f * half_rows + i] + s).astype(jnp.float32),
                    position,
                )
        angle = position * freq[...]
        cosines.append(jnp.cos(angle))
        sines.append(jnp.where(lane < HD // 2, -jnp.sin(angle), jnp.sin(angle)))

    def settle(n, f):
        arrived(from_along.at[n, f], along_recv.at[n, f])
        span = slice(f * half, (f + 1) * half)
        for h in range(chunk_heads):
            columns = slice(h * HD, (h + 1) * HD)
            total = prod[n, pair, side, span, columns] + from_other[n, pair, span, columns]
            for d in range(pairs - 1):
                total = total + from_along[n, f, d, :, columns].astype(jnp.float32)
            total = total * sq[0, 0, span, :]
            for z in range(inner):
                mixed[z, h * tile : (h + 1) * tile, :] = total[z * tile : (z + 1) * tile]
        for z in range(inner):
            to_across[n, f, z] = (
                mixed[z].reshape(chunk_heads // per_tile, SUB, HD).astype(jnp.bfloat16)
            )
        for d in range(inner - 1):
            send_across(n, f, d).start()
        keep_own(n, f).start()

    early = chunks // 2

    @pl.loop(0, chunks)
    def _(n):
        settle(n, 0)

    @pl.loop(0, early)
    def _(n):
        settle(n, 1)

    upper = lax.broadcasted_iota(jnp.int32, (SUB, HD), 0) < tile
    queries = size // per_tile
    kv_heads = inner * groups
    columns = kv_heads * STEPS * size
    slot = lax.broadcasted_iota(jnp.int32, (slots + EXTRA, columns), 0)
    column = lax.broadcasted_iota(jnp.int32, (1, columns), 1)
    newest = jnp.where(lax.rem(column, STEPS * size) >= size, slots + 1, slots)

    def forward(f, d):
        for e in range(pairs - 1):
            gather(f, d, e).start()

    def forward_all(f):
        keep_rows(f).wait()
        forward(f, 0)
        for d in range(1, inner):
            send_rows(f, d - 1).wait_recv()
            forward(f, d)
        share(f, 0).start()

    fresh[...] = jnp.zeros_like(fresh)

    @pl.loop(0, half_rows)
    def _(i):
        spread[i] = jnp.zeros(spread.shape[1:], jnp.bfloat16)

    for copy in kv_copies:
        copy.wait()

    for f in range(HALVES):

        @pl.loop(0, chunks)
        def _(n):
            if f > 0:

                @pl.when(n >= early)
                def _():
                    settle(n, f)

        arrived(joined.at[0, :, f], own_sem.at[f])
        arrived(joined.at[pl.ds(0, inner - 1), :, f], across_recv.at[f])

        if f > 0:
            forward_all(f - 1)

        @pl.loop(0, inner)
        def _(y):
            here_now = joined[y, :, f].reshape(groups * per * tile // SUB, SUB, HD)
            for j in range(groups):
                k = y * groups + j
                turn = here_now[j * per * tile // SUB : (j + 1) * per * tile // SUB]
                turn = turn.astype(jnp.float32)
                turned_now = turn * cosines[f][None] + pltpu.roll(turn, HD // 2, 2) * sines[f][None]
                turned_now = turned_now.astype(jnp.bfloat16).astype(jnp.float32)
                turned[j, : size * tile] = turned_now[:queries].reshape(size * tile, HD)
                turned[j, size * tile :] = jnp.where(upper, turned_now[queries], turn[queries])
                place = pl.ds(pl.multiple_of(k * HD, HD), HD)
                band = pl.ds(pl.multiple_of(k * STEPS * size, STEPS * size), STEPS * size)
                for i in range(half_rows):
                    query = jnp.concatenate(
                        [
                            turned[j, pl.ds(s * half_rows + i, size, stride=tile), :]
                            for s in range(STEPS)
                        ],
                        axis=0,
                    )
                    spread[i, band, place] = query.astype(jnp.bfloat16)
                    for s in range(STEPS):
                        for c in range(2):
                            row = (size + c) * tile + s * half_rows + i
                            fresh[i, c, s : s + 1, place] = turned[j, row : row + 1, :]

        for i in range(half_rows):
            row = f * half_rows + i
            k_here[row, slots:, :] = fresh[i, 0].astype(jnp.bfloat16)
            v_here[row, slots:, :] = fresh[i, 1].astype(jnp.bfloat16)
            scores = (
                lax.dot_general(
                    k_here[row],
                    spread[i],
                    (((1,), (1,)), ((), ())),
                    preferred_element_type=jnp.float32,
                )
                * scale
            )
            valid = (slot < lengths[row]) | ((slot >= slots) & (slot <= newest))
            scores = jnp.where(valid, scores, -jnp.inf)
            soft = jnp.exp(scores - jnp.max(scores, axis=0, keepdims=True))
            total = jnp.sum(soft, axis=0, keepdims=True)
            total = jnp.broadcast_to(total, (SUB, columns)).T
            soft = soft.astype(jnp.bfloat16).T
            for k in range(kv_heads):
                band = slice(k * STEPS * size, (k + 1) * STEPS * size)
                blend = jnp.dot(
                    soft[band],
                    v_here[row, :, k * HD : (k + 1) * HD],
                    preferred_element_type=jnp.float32,
                )
                blend = blend / total[band, 0:1]
                for s in range(STEPS):
                    mix[k, pl.ds(s * half_rows + i, size, stride=tile), :] = blend[
                        s * size : (s + 1) * size
                    ]

        for d in range(inner):
            there = lax.rem(gy + d + 1, inner)
            for j in range(groups):
                to_rows[f, d, j] = (
                    mix[there * groups + j].reshape(queries, SUB, HD).astype(jnp.bfloat16)
                )
            if d < inner - 1:
                send_rows(f, d).start()
        keep_rows(f).start()

    heads_piece = depth // HD
    span = inner * tile

    def pass_side(f):
        for e in range(pairs - 1):
            arrived(held.at[f, 0], gather_recv.at[f, e])
            share(f, e + 1).start()

    def bring(f):
        for e in range(pairs):
            share(f, e).wait_recv()

        @pl.loop(0, outer)
        def _(g):
            place = pl.ds(pl.multiple_of(g * span, span), span)
            for j in range(groups):
                for q in range(queries):
                    both = held[f, g, :, j, q].astype(jnp.float32)
                    for t in range(per_tile):
                        for z in range(inner):
                            parted[q, t, z * tile : (z + 1) * tile, :] = both[
                                z, t * tile : (t + 1) * tile
                            ]
                    for t in range(per_tile):
                        head = j * size + q * per_tile + t
                        column = (head % heads_piece) * HD
                        flat[f, head // heads_piece, place, column : column + HD] = parted[
                            q, t
                        ].astype(jnp.bfloat16)

    for f in range(HALVES):
        if f < HALVES - 1:
            pass_side(f)
        if f == max(HALVES - 2, 0):
            forward_all(HALVES - 1)
        if f == HALVES - 1:
            pass_side(f)
        bring(f)

        @pl.loop(0, out_blocks)
        def _(n):
            total = None
            if f == 0:
                out_ready(n).wait()
            for p in range(pieces):
                product = jnp.dot(
                    flat[f, p], weights[n * pieces + p], preferred_element_type=jnp.float32
                )
                total = product if total is None else total + product
            own[f, n] = total.reshape(inner, part, cw)
            for d in range(inner - 1):
                to_sum[f, n, d] = own[f, n, lax.rem(gy + d + 1, inner)].astype(jnp.bfloat16)
                send_sum(f, n, d).start()

    for f in range(HALVES):

        @pl.loop(0, out_blocks)
        def _(n):
            arrived(from_sum.at[f, n], sum_recv.at[f, n])
            for c in range(cw // HD):
                columns = slice(c * HD, (c + 1) * HD)
                total = own[f, n, gy, :, columns]
                for d in range(inner - 1):
                    total = total + from_sum[f, n, d, :, columns].astype(jnp.float32)
                for q in range(part // tile):
                    for s in range(STEPS):
                        start = q * tile + s * half_rows
                        target = q * rows + f * half_rows
                        place = pl.ds(pl.multiple_of(n * cw + c * HD, HD), HD)
                        piece[s, target : target + half_rows, place] = total[
                            start : start + half_rows
                        ]

    for s in range(STEPS):
        result[s] = piece[s].astype(jnp.bfloat16)

    arrived(prod.at[:, :, 0], pair_send)
    arrived(sq_to, sqa_send)
    for f in range(HALVES):
        arrived(to_along.at[:, f], along_send.at[f])
        arrived(to_across.at[:, f, pl.ds(0, inner - 1)], across_send.at[f])
        arrived(to_rows.at[f, pl.ds(0, inner - 1)], rows_send.at[f])
        arrived(held.at[f, pl.ds(0, pairs - 1)], gather_send.at[f])
        arrived(held.at[f, pl.ds(0, pairs)], share_send.at[f])
        arrived(to_sum.at[f], sum_send.at[f])


def body(x_first, x_second, norm_gain, w_qkv, w_out, cache_keys, cache_values, lengths):
    outer, inner = lax.axis_size("gx"), lax.axis_size("gy")
    rows, slots, kv_width = cache_keys.shape
    depth, in_columns = w_qkv.shape
    out_depth, out_columns = w_out.shape
    width = depth * outer
    heads = in_columns // HD
    groups = kv_width // HD // inner
    size = heads // groups - 2
    chunk_heads = 4 if in_columns % (4 * HD) == 0 and out_columns % (4 * HD) == 0 else 2
    chunks = heads // chunk_heads
    cw = chunk_heads * HD
    pairs = outer // 2
    here = STEPS * inner * rows
    tile = STEPS * rows // HALVES
    queries = size * tile // SUB
    total = outer * here // HALVES
    part = total // inner
    out_blocks = out_columns // cw
    pieces = out_depth // depth
    dims = (outer, inner, rows, width, groups, size, chunk_heads, chunks)

    half = HD // 2
    freq = rotary_base ** (-(np.arange(half, dtype=np.float64) * 2.0 / HD))
    freq = jnp.asarray(np.tile(freq, 2)[None], jnp.float32)

    dma = pltpu.SemaphoreType.DMA
    vmem = pl.BlockSpec(memory_space=pltpu.VMEM)
    away = pl.BlockSpec(memory_space=pl.ANY)
    f32, b16 = jnp.float32, jnp.bfloat16
    result = pl.pallas_call(
        functools.partial(block_kernel, dims),
        in_specs=[
            pl.BlockSpec(memory_space=pltpu.SMEM), away, away, vmem, vmem, away, away, away, away,
        ],
        out_specs=vmem,
        out_shape=jax.ShapeDtypeStruct((STEPS, HALVES * part // STEPS, out_columns), b16),
        scratch_shapes=[
            pltpu.VMEM((STEPS, outer * inner * rows, depth), b16),
            pltpu.VMEM((rows, slots + EXTRA, kv_width), b16),
            pltpu.VMEM((rows, slots + EXTRA, kv_width), b16),
            pltpu.VMEM((max(in_columns // cw, out_blocks * pieces), depth, cw), b16),
            pltpu.VMEM((outer * here, depth), b16),
            pltpu.VMEM((chunks, pairs, 2, here, cw), f32),
            pltpu.VMEM((chunks, pairs, here, cw), f32),
            pltpu.VMEM((chunks, HALVES, pairs - 1, here // HALVES, cw), b16),
            pltpu.VMEM((chunks, HALVES, pairs - 1, here // HALVES, cw), b16),
            pltpu.VMEM((pairs, 2, here, HD), f32),
            pltpu.VMEM((pairs, here, HD), f32),
            pltpu.VMEM((pairs - 1, here, HD), f32),
            pltpu.VMEM((pairs - 1, here, HD), f32),
            pltpu.VMEM((inner, chunk_heads * tile, HD), f32),
            pltpu.VMEM((chunks, HALVES, inner, chunk_heads * tile // SUB, SUB, HD), b16),
            pltpu.VMEM((inner, chunks, HALVES, chunk_heads * tile // SUB, SUB, HD), b16),
            pltpu.VMEM((groups, (size + 2) * tile, HD), f32),
            pltpu.VMEM((rows // HALVES, kv_width // HD * STEPS * size, kv_width), b16),
            pltpu.VMEM((rows // HALVES, 2, EXTRA, kv_width), f32),
            pltpu.VMEM((kv_width // HD, size * tile, HD), f32),
            pltpu.VMEM((HALVES, inner, groups, queries, SUB, HD), b16),
            pltpu.VMEM((HALVES, outer, inner, groups, queries, SUB, HD), b16),
            pltpu.VMEM((queries, SUB // tile, inner * tile, HD), f32),
            pltpu.VMEM((HALVES, pieces, total, depth), b16),
            pltpu.VMEM((HALVES, out_blocks, inner, part, cw), f32),
            pltpu.VMEM((HALVES, out_blocks, inner - 1, part, cw), b16),
            pltpu.VMEM((HALVES, out_blocks, inner - 1, part, cw), b16),
            pltpu.VMEM((STEPS, HALVES * part // STEPS, out_columns), f32),
            dma((STEPS,)), dma((2,)), dma((chunks,)), dma((out_blocks,)),
            dma, dma((chunks,)),
            dma((HALVES,)), dma((chunks, HALVES)),
            dma((HALVES,)), dma((HALVES,)),
            dma, dma, dma, dma, dma((HALVES,)),
            dma((HALVES,)), dma((HALVES, inner - 1)), dma((HALVES,)),
            dma((HALVES,)), dma((HALVES, pairs - 1)),
            dma((HALVES,)), dma((HALVES, pairs)),
            dma((HALVES,)), dma((HALVES, out_blocks)),
        ],
        compiler_params=pltpu.CompilerParams(
            collective_id=0, has_side_effects=True, vmem_limit_bytes=VMEM_LIMIT
        ),
        name="decode_block",
    )(lengths, x_first, x_second, norm_gain, freq, w_qkv, w_out, cache_keys, cache_values)
    return result[0], result[1]


def solution(mesh):
    in_specs = (
        P(None, "gx"),
        P(None, "gx"),
        P("gx"),
        P("gx", "gy"),
        P("gy", "gx"),
        P(("gx", "gy"), None, None),
        P(("gx", "gy"), None, None),
        P(("gx", "gy")),
    )
    out_specs = (P("gy", "gx"), P("gy", "gx"))
    return jax.shard_map(body, mesh=mesh, in_specs=in_specs, out_specs=out_specs, check_vma=False)
```

```python
import functools
import math

import jax
import jax.numpy as jnp
import numpy as np
from jax import lax
from jax.experimental import pallas as pl
from jax.experimental.pallas import tpu as pltpu
from jax.sharding import PartitionSpec as P

HD = 128
norm_eps = 1e-05
rotary_base = 500000.0
STEPS = 2
HALVES = 2
SUB = 8
EXTRA = 16
LAG = 2
VMEM_LIMIT = 62 * 1024 * 1024
MESH = pl.DeviceIdType.MESH


def remote(src, dst, send, recv, device):
    return pltpu.make_async_remote_copy(
        src_ref=src, dst_ref=dst, send_sem=send, recv_sem=recv,
        device_id=device, device_id_type=MESH,
    )


def block_kernel(
    dims, lengths, x_first, x_second, gain, freq, w_in, w_out, keys, values, result,
    x_here, k_here, v_here, weights, scaled, prod, from_other, to_along, from_along,
    sq, sq_other, sq_to, sq_along, mixed, to_across, joined,
    turned, spread, fresh, mix, to_rows, held, parted, flat, own, to_sum, from_sum, piece,
    x_sem, kv_sem, in_sem, out_sem, pair_send, pair_recv, along_send, along_recv,
    across_send, across_recv, sq_send, sq_recv, sqa_send, sqa_recv, own_sem,
    rows_send, rows_recv, keep_sem, gather_send, gather_recv, share_send, share_recv,
    sum_send, sum_recv,
):
    outer, inner, rows, width, groups, size, chunk_heads, chunks = dims
    gx, gy = lax.axis_index("gx"), lax.axis_index("gy")
    pairs = outer // 2
    pair, side = gx // 2, lax.rem(gx, 2)
    other = (gx + 1 - 2 * side, gy)
    along = [(2 * lax.rem(pair + d, pairs) + side, gy) for d in range(1, pairs)]
    across = [(gx, lax.rem(gy + d, inner)) for d in range(1, inner)]
    cw = chunk_heads * HD
    block = inner * rows
    here = STEPS * block
    half_rows = rows // HALVES
    tile = STEPS * half_rows
    per_tile = SUB // tile
    per = size + 2
    slots = k_here.shape[1] - EXTRA
    half = here // HALVES
    depth = scaled.shape[1]
    out_blocks = own.shape[1]
    pieces = flat.shape[1]
    part = own.shape[3]
    scale = 1.0 / math.sqrt(HD)

    x_copies = [
        pltpu.make_async_copy(x, x_here.at[s], x_sem.at[s])
        for s, x in enumerate((x_first, x_second))
    ]

    def in_copy(b):
        return pltpu.make_async_copy(
            w_in.at[:, pl.ds(pl.multiple_of(b * cw, cw), cw)], weights.at[b], in_sem.at[b]
        )

    def out_copy(n, p):
        return pltpu.make_async_copy(
            w_out.at[
                pl.ds(p * depth, depth), pl.ds(pl.multiple_of(n * cw, cw), cw)
            ],
            weights.at[n * pieces + p],
            out_sem.at[n],
        )

    def out_ready(n):
        ref = weights.at[pl.ds(n * pieces, pieces)]
        return pltpu.make_async_copy(ref, ref, out_sem.at[n])

    kv_copies = [
        pltpu.make_async_copy(keys, k_here.at[:, pl.ds(0, slots)], kv_sem.at[0]),
        pltpu.make_async_copy(values, v_here.at[:, pl.ds(0, slots)], kv_sem.at[1]),
    ]

    def send_sq():
        return remote(sq.at[:, 1 - side], sq_other, sq_send, sq_recv, other)

    def send_sq_along(d):
        return remote(sq_to.at[d], sq_along.at[d], sqa_send, sqa_recv, along[d])

    def send_pair(n):
        return remote(
            prod.at[n, :, 1 - side], from_other.at[n], pair_send, pair_recv.at[n], other
        )

    def send_along(n, f, d):
        return remote(
            to_along.at[n, f, d], from_along.at[n, f, d],
            along_send.at[f], along_recv.at[n, f], along[d],
        )

    def send_across(n, f, d):
        return remote(
            to_across.at[n, f, lax.rem(gy + d + 1, inner)], joined.at[gy, n, f],
            across_send.at[f], across_recv.at[f], across[d],
        )

    def keep_own(n, f):
        return pltpu.make_async_copy(
            to_across.at[n, f, gy], joined.at[gy, n, f], own_sem.at[f]
        )

    def source(d):
        return lax.rem(gy + inner - d, inner)

    def send_rows(f, d):
        return remote(
            to_rows.at[f, d], held.at[f, gx, gy], rows_send.at[f], rows_recv.at[f, d], across[d]
        )

    def keep_rows(f):
        return pltpu.make_async_copy(
            to_rows.at[f, inner - 1], held.at[f, gx, gy], keep_sem.at[f]
        )

    def gather(f, d, e):
        ref = held.at[f, gx, source(d)]
        return remote(ref, ref, gather_send.at[f], gather_recv.at[f, e], along[e])

    def share(f, e):
        ref = held.at[f, 2 * lax.rem(pair + pairs - e, pairs) + side]
        return remote(ref, ref, share_send.at[f], share_recv.at[f, e], other)

    def send_sum(f, n, d):
        return remote(
            to_sum.at[f, n, d], from_sum.at[f, n, d],
            sum_send.at[f], sum_recv.at[f, n], across[d],
        )

    def arrived(ref, sem):
        pltpu.make_async_copy(ref, ref, sem).wait()

    for copy in x_copies:
        copy.start()

    @pl.loop(0, chunks)
    def _(b):
        in_copy(b).start()

    for copy in kv_copies:
        copy.start()

    barrier = pltpu.get_barrier_semaphore()
    peers = [other] + along + across
    for peer in peers:
        pl.semaphore_signal(barrier, inc=1, device_id=peer, device_id_type=MESH)

    to = lax.broadcasted_iota(jnp.int32, (here, here), 0)
    step = lax.rem(lax.div(to, half_rows), STEPS)
    member = lax.rem(lax.div(to, tile), inner)
    start = lax.div(to, half) * half_rows + lax.rem(to, half_rows)
    source_row = step * block + member * rows + start
    order = jnp.where(
        source_row == lax.broadcasted_iota(jnp.int32, (here, here), 1), 1.0, 0.0
    ).astype(jnp.bfloat16)
    wide_gain = gain[...].astype(jnp.float32).reshape(1, depth)
    for copy in x_copies:
        copy.wait()

    @pl.loop(0, outer)
    def _(g):
        parts = []
        for s in range(STEPS):
            wide = x_here[s, pl.ds(pl.multiple_of(g * block, block), block), :].astype(jnp.float32)
            parts.append((wide * wide_gain).astype(jnp.bfloat16))
            total = jnp.sum(wide * wide, axis=1, keepdims=True)
            sq[g // 2, lax.rem(g, 2), s * block : (s + 1) * block, :] = jnp.broadcast_to(
                total, (block, HD)
            )
        scaled[pl.ds(pl.multiple_of(g * here, here), here), :] = jnp.dot(
            order, jnp.concatenate(parts, axis=0), preferred_element_type=jnp.float32
        ).astype(jnp.bfloat16)

    pl.semaphore_wait(barrier, len(peers))
    send_sq().start()

    def pass_on(n):
        send_pair(n).wait_recv()
        for d in range(pairs - 1):
            there = lax.rem(pair + d + 1, pairs)
            both = (prod[n, there, side] + from_other[n, there]).astype(jnp.bfloat16)
            for f in range(HALVES):
                to_along[n, f, d] = both[f * half : (f + 1) * half]
            send_along(n, 0, d).start()

    @pl.loop(0, chunks)
    def _(n):
        in_copy(n).wait()
        product = jnp.dot(scaled[...], weights[n], preferred_element_type=jnp.float32)
        prod[n] = product.reshape(pairs, 2, here, cw)
        send_pair(n).start()

        @pl.when(n == 0)
        def _():
            send_sq().wait()
            for d in range(pairs - 1):
                there = lax.rem(pair + d + 1, pairs)
                sq_to[d] = sq[there, side] + sq_other[there]
                send_sq_along(d).start()

        @pl.when(n >= LAG)
        def _():
            pass_on(n - LAG)

    @pl.loop(chunks - LAG, chunks)
    def _(n):
        pass_on(n)

    @pl.loop(0, chunks)
    def _(n):
        for f in range(1, HALVES):
            for d in range(pairs - 1):
                send_along(n, f, d).start()

    @pl.loop(0, out_blocks)
    def _(n):
        for p in range(pieces):
            out_copy(n, p).start()

    squares = sq[pair, side] + sq_other[pair]
    arrived(sq_along, sqa_recv)
    for d in range(pairs - 1):
        squares = squares + sq_along[d]
    factor = lax.rsqrt(squares / width + norm_eps)
    for f in range(HALVES):
        for z in range(inner):
            for s in range(STEPS):
                target = f * half + z * tile + s * half_rows
                row = s * block + z * rows + f * half_rows
                sq[0, 0, target : target + half_rows, :] = factor[row : row + half_rows]

    index = lax.rem(lax.broadcasted_iota(jnp.int32, (SUB, HD), 0), tile)
    lane = lax.broadcasted_iota(jnp.int32, (SUB, HD), 1)
    cosines, sines = [], []
    for f in range(HALVES):
        position = jnp.zeros((SUB, HD), jnp.float32)
        for s in range(STEPS):
            for i in range(half_rows):
                position = jnp.where(
                    index == s * half_rows + i,
                    (lengths[f * half_rows + i] + s).astype(jnp.float32),
                    position,
                )
        angle = position * freq[...]
        cosines.append(jnp.cos(angle))
        sines.append(jnp.where(lane < HD // 2, -jnp.sin(angle), jnp.sin(angle)))

    def settle(n, f):
        arrived(from_along.at[n, f], along_recv.at[n, f])
        span = slice(f * half, (f + 1) * half)
        for h in range(chunk_heads):
            columns = slice(h * HD, (h + 1) * HD)
            total = prod[n, pair, side, span, columns] + from_other[n, pair, span, columns]
            for d in range(pairs - 1):
                total = total + from_along[n, f, d, :, columns].astype(jnp.float32)
            total = total * sq[0, 0, span, :]
            for z in range(inner):
                mixed[z, h * tile : (h + 1) * tile, :] = total[z * tile : (z + 1) * tile]
        for z in range(inner):
            to_across[n, f, z] = (
                mixed[z].reshape(chunk_heads // per_tile, SUB, HD).astype(jnp.bfloat16)
            )
        for d in range(inner - 1):
            send_across(n, f, d).start()
        keep_own(n, f).start()

    early = chunks // 2

    @pl.loop(0, chunks)
    def _(n):
        settle(n, 0)

    @pl.loop(0, early)
    def _(n):
        settle(n, 1)

    upper = lax.broadcasted_iota(jnp.int32, (SUB, HD), 0) < tile
    queries = size // per_tile
    kv_heads = inner * groups
    columns = kv_heads * STEPS * size
    slot = lax.broadcasted_iota(jnp.int32, (slots + EXTRA, columns), 0)
    column = lax.broadcasted_iota(jnp.int32, (1, columns), 1)
    newest = jnp.where(lax.rem(column, STEPS * size) >= size, slots + 1, slots)

    def forward(f, d):
        for e in range(pairs - 1):
            gather(f, d, e).start()

    def forward_all(f):
        for d in range(1, inner):
            send_rows(f, d - 1).wait_recv()
            forward(f, d)
        share(f, 0).start()

    fresh[...] = jnp.zeros_like(fresh)

    @pl.loop(0, half_rows)
    def _(i):
        spread[i] = jnp.zeros(spread.shape[1:], jnp.bfloat16)

    for copy in kv_copies:
        copy.wait()

    for f in range(HALVES):

        @pl.loop(0, chunks)
        def _(n):
            if f > 0:

                @pl.when(n >= early)
                def _():
                    settle(n, f)

        if f > 0:
            forward_all(f - 1)
        arrived(joined.at[0, :, f], own_sem.at[f])
        arrived(joined.at[pl.ds(0, inner - 1), :, f], across_recv.at[f])

        @pl.loop(0, inner)
        def _(y):
            here_now = joined[y, :, f].reshape(groups * per * tile // SUB, SUB, HD)
            for j in range(groups):
                k = y * groups + j
                turn = here_now[j * per * tile // SUB : (j + 1) * per * tile // SUB]
                turn = turn.astype(jnp.float32)
                turned_now = turn * cosines[f][None] + pltpu.roll(turn, HD // 2, 2) * sines[f][None]
                turned_now = turned_now.astype(jnp.bfloat16).astype(jnp.float32)
                turned[j, : size * tile] = turned_now[:queries].reshape(size * tile, HD)
                turned[j, size * tile :] = jnp.where(upper, turned_now[queries], turn[queries])
                place = pl.ds(pl.multiple_of(k * HD, HD), HD)
                band = pl.ds(pl.multiple_of(k * STEPS * size, STEPS * size), STEPS * size)
                for i in range(half_rows):
                    query = jnp.concatenate(
                        [
                            turned[j, pl.ds(s * half_rows + i, size, stride=tile), :]
                            for s in range(STEPS)
                        ],
                        axis=0,
                    )
                    spread[i, band, place] = query.astype(jnp.bfloat16)
                    for s in range(STEPS):
                        for c in range(2):
                            row = (size + c) * tile + s * half_rows + i
                            fresh[i, c, s : s + 1, place] = turned[j, row : row + 1, :]

        for i in range(half_rows):
            row = f * half_rows + i
            k_here[row, slots:, :] = fresh[i, 0].astype(jnp.bfloat16)
            v_here[row, slots:, :] = fresh[i, 1].astype(jnp.bfloat16)
            scores = (
                lax.dot_general(
                    k_here[row],
                    spread[i],
                    (((1,), (1,)), ((), ())),
                    preferred_element_type=jnp.float32,
                )
                * scale
            )
            valid = (slot < lengths[row]) | ((slot >= slots) & (slot <= newest))
            scores = jnp.where(valid, scores, -jnp.inf)
            soft = jnp.exp(scores - jnp.max(scores, axis=0, keepdims=True))
            total = jnp.sum(soft, axis=0, keepdims=True)
            total = jnp.broadcast_to(total, (SUB, columns)).T
            soft = soft.astype(jnp.bfloat16).T
            for k in range(kv_heads):
                band = slice(k * STEPS * size, (k + 1) * STEPS * size)
                blend = jnp.dot(
                    soft[band],
                    v_here[row, :, k * HD : (k + 1) * HD],
                    preferred_element_type=jnp.float32,
                )
                blend = blend / total[band, 0:1]
                for s in range(STEPS):
                    mix[k, pl.ds(s * half_rows + i, size, stride=tile), :] = blend[
                        s * size : (s + 1) * size
                    ]

        for d in range(inner):
            there = lax.rem(gy + d + 1, inner)
            for j in range(groups):
                to_rows[f, d, j] = (
                    mix[there * groups + j].reshape(queries, SUB, HD).astype(jnp.bfloat16)
                )
            if d < inner - 1:
                send_rows(f, d).start()
        keep_rows(f).start()
        keep_rows(f).wait()
        forward(f, 0)

    heads_piece = depth // HD
    span = inner * tile

    def pass_side(f):
        for e in range(pairs - 1):
            arrived(held.at[f, 0], gather_recv.at[f, e])
            share(f, e + 1).start()

    def bring(f):
        for e in range(pairs):
            share(f, e).wait_recv()

        @pl.loop(0, outer)
        def _(g):
            place = pl.ds(pl.multiple_of(g * span, span), span)
            for j in range(groups):
                for q in range(queries):
                    both = held[f, g, :, j, q].astype(jnp.float32)
                    for t in range(per_tile):
                        for z in range(inner):
                            parted[q, t, z * tile : (z + 1) * tile, :] = both[
                                z, t * tile : (t + 1) * tile
                            ]
                    for t in range(per_tile):
                        head = j * size + q * per_tile + t
                        column = (head % heads_piece) * HD
                        flat[f, head // heads_piece, place, column : column + HD] = parted[
                            q, t
                        ].astype(jnp.bfloat16)

    for f in range(HALVES):
        if f < HALVES - 1:
            pass_side(f)
        if f == max(HALVES - 2, 0):
            forward_all(HALVES - 1)
        if f == HALVES - 1:
            pass_side(f)
        bring(f)

        @pl.loop(0, out_blocks)
        def _(n):
            total = None
            if f == 0:
                out_ready(n).wait()
            for p in range(pieces):
                product = jnp.dot(
                    flat[f, p], weights[n * pieces + p], preferred_element_type=jnp.float32
                )
                total = product if total is None else total + product
            own[f, n] = total.reshape(inner, part, cw)
            for d in range(inner - 1):
                to_sum[f, n, d] = own[f, n, lax.rem(gy + d + 1, inner)].astype(jnp.bfloat16)
                send_sum(f, n, d).start()

    for f in range(HALVES):

        @pl.loop(0, out_blocks)
        def _(n):
            arrived(from_sum.at[f, n], sum_recv.at[f, n])
            for c in range(cw // HD):
                columns = slice(c * HD, (c + 1) * HD)
                total = own[f, n, gy, :, columns]
                for d in range(inner - 1):
                    total = total + from_sum[f, n, d, :, columns].astype(jnp.float32)
                for q in range(part // tile):
                    for s in range(STEPS):
                        start = q * tile + s * half_rows
                        target = q * rows + f * half_rows
                        place = pl.ds(pl.multiple_of(n * cw + c * HD, HD), HD)
                        piece[s, target : target + half_rows, place] = total[
                            start : start + half_rows
                        ]
                if f == HALVES - 1:
                    for s in range(STEPS):
                        result[s, :, place] = piece[s, :, place].astype(jnp.bfloat16)

    arrived(prod.at[:, :, 0], pair_send)
    arrived(sq_to, sqa_send)
    for f in range(HALVES):
        arrived(to_along.at[:, f], along_send.at[f])
        arrived(to_across.at[:, f, pl.ds(0, inner - 1)], across_send.at[f])
        arrived(to_rows.at[f, pl.ds(0, inner - 1)], rows_send.at[f])
        arrived(held.at[f, pl.ds(0, pairs - 1)], gather_send.at[f])
        arrived(held.at[f, pl.ds(0, pairs)], share_send.at[f])
        arrived(to_sum.at[f], sum_send.at[f])


def body(x_first, x_second, norm_gain, w_qkv, w_out, cache_keys, cache_values, lengths):
    outer, inner = lax.axis_size("gx"), lax.axis_size("gy")
    rows, slots, kv_width = cache_keys.shape
    depth, in_columns = w_qkv.shape
    out_depth, out_columns = w_out.shape
    width = depth * outer
    heads = in_columns // HD
    groups = kv_width // HD // inner
    size = heads // groups - 2
    chunk_heads = 4 if in_columns % (4 * HD) == 0 and out_columns % (4 * HD) == 0 else 2
    chunks = heads // chunk_heads
    cw = chunk_heads * HD
    pairs = outer // 2
    here = STEPS * inner * rows
    tile = STEPS * rows // HALVES
    queries = size * tile // SUB
    total = outer * here // HALVES
    part = total // inner
    out_blocks = out_columns // cw
    pieces = out_depth // depth
    dims = (outer, inner, rows, width, groups, size, chunk_heads, chunks)

    half = HD // 2
    freq = rotary_base ** (-(np.arange(half, dtype=np.float64) * 2.0 / HD))
    freq = jnp.asarray(np.tile(freq, 2)[None], jnp.float32)

    dma = pltpu.SemaphoreType.DMA
    vmem = pl.BlockSpec(memory_space=pltpu.VMEM)
    away = pl.BlockSpec(memory_space=pl.ANY)
    f32, b16 = jnp.float32, jnp.bfloat16
    result = pl.pallas_call(
        functools.partial(block_kernel, dims),
        in_specs=[
            pl.BlockSpec(memory_space=pltpu.SMEM), away, away, vmem, vmem, away, away, away, away,
        ],
        out_specs=vmem,
        out_shape=jax.ShapeDtypeStruct((STEPS, HALVES * part // STEPS, out_columns), b16),
        scratch_shapes=[
            pltpu.VMEM((STEPS, outer * inner * rows, depth), b16),
            pltpu.VMEM((rows, slots + EXTRA, kv_width), b16),
            pltpu.VMEM((rows, slots + EXTRA, kv_width), b16),
            pltpu.VMEM((max(in_columns // cw, out_blocks * pieces), depth, cw), b16),
            pltpu.VMEM((outer * here, depth), b16),
            pltpu.VMEM((chunks, pairs, 2, here, cw), f32),
            pltpu.VMEM((chunks, pairs, here, cw), f32),
            pltpu.VMEM((chunks, HALVES, pairs - 1, here // HALVES, cw), b16),
            pltpu.VMEM((chunks, HALVES, pairs - 1, here // HALVES, cw), b16),
            pltpu.VMEM((pairs, 2, here, HD), f32),
            pltpu.VMEM((pairs, here, HD), f32),
            pltpu.VMEM((pairs - 1, here, HD), f32),
            pltpu.VMEM((pairs - 1, here, HD), f32),
            pltpu.VMEM((inner, chunk_heads * tile, HD), f32),
            pltpu.VMEM((chunks, HALVES, inner, chunk_heads * tile // SUB, SUB, HD), b16),
            pltpu.VMEM((inner, chunks, HALVES, chunk_heads * tile // SUB, SUB, HD), b16),
            pltpu.VMEM((groups, (size + 2) * tile, HD), f32),
            pltpu.VMEM((rows // HALVES, kv_width // HD * STEPS * size, kv_width), b16),
            pltpu.VMEM((rows // HALVES, 2, EXTRA, kv_width), f32),
            pltpu.VMEM((kv_width // HD, size * tile, HD), f32),
            pltpu.VMEM((HALVES, inner, groups, queries, SUB, HD), b16),
            pltpu.VMEM((HALVES, outer, inner, groups, queries, SUB, HD), b16),
            pltpu.VMEM((queries, SUB // tile, inner * tile, HD), f32),
            pltpu.VMEM((HALVES, pieces, total, depth), b16),
            pltpu.VMEM((HALVES, out_blocks, inner, part, cw), f32),
            pltpu.VMEM((HALVES, out_blocks, inner - 1, part, cw), b16),
            pltpu.VMEM((HALVES, out_blocks, inner - 1, part, cw), b16),
            pltpu.VMEM((STEPS, HALVES * part // STEPS, out_columns), f32),
            dma((STEPS,)), dma((2,)), dma((chunks,)), dma((out_blocks,)),
            dma, dma((chunks,)),
            dma((HALVES,)), dma((chunks, HALVES)),
            dma((HALVES,)), dma((HALVES,)),
            dma, dma, dma, dma, dma((HALVES,)),
            dma((HALVES,)), dma((HALVES, inner - 1)), dma((HALVES,)),
            dma((HALVES,)), dma((HALVES, pairs - 1)),
            dma((HALVES,)), dma((HALVES, pairs)),
            dma((HALVES,)), dma((HALVES, out_blocks)),
        ],
        compiler_params=pltpu.CompilerParams(
            collective_id=0, has_side_effects=True, vmem_limit_bytes=VMEM_LIMIT
        ),
        name="decode_block",
    )(lengths, x_first, x_second, norm_gain, freq, w_qkv, w_out, cache_keys, cache_values)
    return result[0], result[1]


def solution(mesh):
    in_specs = (
        P(None, "gx"),
        P(None, "gx"),
        P("gx"),
        P("gx", "gy"),
        P("gy", "gx"),
        P(("gx", "gy"), None, None),
        P(("gx", "gy"), None, None),
        P(("gx", "gy")),
    )
    out_specs = (P("gy", "gx"), P("gy", "gx"))
    return jax.shard_map(body, mesh=mesh, in_specs=in_specs, out_specs=out_specs, check_vma=False)
```

```python
import functools
import math

import jax
import jax.numpy as jnp
import numpy as np
from jax import lax
from jax.experimental import pallas as pl
from jax.experimental.pallas import tpu as pltpu
from jax.sharding import PartitionSpec as P

HD = 128
norm_eps = 1e-05
rotary_base = 500000.0
STEPS = 2
HALVES = 2
SUB = 8
EXTRA = 16
LAG = 2
RELAYS = (2, 2)
VMEM_LIMIT = 62 * 1024 * 1024
MESH = pl.DeviceIdType.MESH


def remote(src, dst, send, recv, device):
    return pltpu.make_async_remote_copy(
        src_ref=src, dst_ref=dst, send_sem=send, recv_sem=recv,
        device_id=device, device_id_type=MESH,
    )


def relays_of(inner, out_blocks):
    return RELAYS if inner == 4 and out_blocks > max(RELAYS) else (0,) * HALVES


def block_kernel(
    dims, lengths, x_first, x_second, gain, freq, w_in, w_out, keys, values, result,
    x_here, k_here, v_here, weights, scaled, prod, from_other, to_along, from_along,
    sq, sq_other, sq_to, sq_along, mixed, to_across, joined,
    turned, spread, fresh, mix, to_rows, held, parted, flat, own, to_sum, from_sum, piece,
    to_near, from_near, wide_near, wide_from, to_far, from_far,
    x_sem, kv_sem, in_sem, out_sem, pair_send, pair_recv, along_send, along_recv,
    across_send, across_recv, sq_send, sq_recv, sqa_send, sqa_recv, own_sem,
    rows_send, rows_recv, keep_sem, gather_send, gather_recv, share_send, share_recv,
    sum_send, sum_recv, near_send, near_recv, wide_send, wide_recv, far_send, far_recv,
):
    outer, inner, rows, width, groups, size, chunk_heads, chunks = dims
    gx, gy = lax.axis_index("gx"), lax.axis_index("gy")
    pairs = outer // 2
    pair, side = gx // 2, lax.rem(gx, 2)
    other = (gx + 1 - 2 * side, gy)
    along = [(2 * lax.rem(pair + d, pairs) + side, gy) for d in range(1, pairs)]
    across = [(gx, lax.rem(gy + d, inner)) for d in range(1, inner)]
    cw = chunk_heads * HD
    block = inner * rows
    here = STEPS * block
    half_rows = rows // HALVES
    tile = STEPS * half_rows
    per_tile = SUB // tile
    per = size + 2
    slots = k_here.shape[1] - EXTRA
    half = here // HALVES
    depth = scaled.shape[1]
    out_blocks = own.shape[1]
    pieces = flat.shape[1]
    part = own.shape[3]
    scale = 1.0 / math.sqrt(HD)

    x_copies = [
        pltpu.make_async_copy(x, x_here.at[s], x_sem.at[s])
        for s, x in enumerate((x_first, x_second))
    ]

    def in_copy(b):
        return pltpu.make_async_copy(
            w_in.at[:, pl.ds(pl.multiple_of(b * cw, cw), cw)], weights.at[b], in_sem.at[b]
        )

    def out_copy(n, p):
        return pltpu.make_async_copy(
            w_out.at[
                pl.ds(p * depth, depth), pl.ds(pl.multiple_of(n * cw, cw), cw)
            ],
            weights.at[n * pieces + p],
            out_sem.at[n],
        )

    def out_ready(n):
        ref = weights.at[pl.ds(n * pieces, pieces)]
        return pltpu.make_async_copy(ref, ref, out_sem.at[n])

    kv_copies = [
        pltpu.make_async_copy(keys, k_here.at[:, pl.ds(0, slots)], kv_sem.at[0]),
        pltpu.make_async_copy(values, v_here.at[:, pl.ds(0, slots)], kv_sem.at[1]),
    ]

    def send_sq():
        return remote(sq.at[:, 1 - side], sq_other, sq_send, sq_recv, other)

    def send_sq_along(d):
        return remote(sq_to.at[d], sq_along.at[d], sqa_send, sqa_recv, along[d])

    def send_pair(n):
        return remote(
            prod.at[n, :, 1 - side], from_other.at[n], pair_send, pair_recv.at[n], other
        )

    def send_along(n, f, d):
        return remote(
            to_along.at[n, f, d], from_along.at[n, f, d],
            along_send.at[f], along_recv.at[n, f], along[d],
        )

    def send_across(n, f, d):
        return remote(
            to_across.at[n, f, lax.rem(gy + d + 1, inner)], joined.at[gy, n, f],
            across_send.at[f], across_recv.at[f], across[d],
        )

    def keep_own(n, f):
        return pltpu.make_async_copy(
            to_across.at[n, f, gy], joined.at[gy, n, f], own_sem.at[f]
        )

    def source(d):
        return lax.rem(gy + inner - d, inner)

    def send_rows(f, d):
        return remote(
            to_rows.at[f, d], held.at[f, gx, gy], rows_send.at[f], rows_recv.at[f, d], across[d]
        )

    def keep_rows(f):
        return pltpu.make_async_copy(
            to_rows.at[f, inner - 1], held.at[f, gx, gy], keep_sem.at[f]
        )

    def gather(f, d, e):
        ref = held.at[f, gx, source(d)]
        return remote(ref, ref, gather_send.at[f], gather_recv.at[f, e], along[e])

    def share(f, e):
        ref = held.at[f, 2 * lax.rem(pair + pairs - e, pairs) + side]
        return remote(ref, ref, share_send.at[f], share_recv.at[f, e], other)

    def send_sum(f, n, d):
        return remote(
            to_sum.at[f, n, d], from_sum.at[f, n, d],
            sum_send.at[f], sum_recv.at[f, n], across[d],
        )

    relays = relays_of(inner, out_blocks)
    near = gy + 1 - 2 * lax.rem(gy, 2)
    near_far, far = lax.rem(near + 2, inner), lax.rem(gy + 2, inner)

    def relay_index(f, n):
        return sum(relays[:f]) + n

    def send_near(k):
        return remote(to_near.at[k], from_near.at[k], near_send, near_recv.at[k], (gx, near))

    def send_wide(k):
        return remote(wide_near.at[k], wide_from.at[k], wide_send, wide_recv.at[k], (gx, near))

    def send_far(k):
        return remote(to_far.at[k], from_far.at[k], far_send, far_recv.at[k], (gx, far))

    def arrived(ref, sem):
        pltpu.make_async_copy(ref, ref, sem).wait()

    for copy in x_copies:
        copy.start()

    @pl.loop(0, chunks)
    def _(b):
        in_copy(b).start()

    for copy in kv_copies:
        copy.start()

    barrier = pltpu.get_barrier_semaphore()
    peers = [other] + along + across
    for peer in peers:
        pl.semaphore_signal(barrier, inc=1, device_id=peer, device_id_type=MESH)

    to = lax.broadcasted_iota(jnp.int32, (here, here), 0)
    step = lax.rem(lax.div(to, half_rows), STEPS)
    member = lax.rem(lax.div(to, tile), inner)
    start = lax.div(to, half) * half_rows + lax.rem(to, half_rows)
    source_row = step * block + member * rows + start
    order = jnp.where(
        source_row == lax.broadcasted_iota(jnp.int32, (here, here), 1), 1.0, 0.0
    ).astype(jnp.bfloat16)
    wide_gain = gain[...].astype(jnp.float32).reshape(1, depth)
    for copy in x_copies:
        copy.wait()

    @pl.loop(0, outer)
    def _(g):
        parts = []
        for s in range(STEPS):
            wide = x_here[s, pl.ds(pl.multiple_of(g * block, block), block), :].astype(jnp.float32)
            parts.append((wide * wide_gain).astype(jnp.bfloat16))
            total = jnp.sum(wide * wide, axis=1, keepdims=True)
            sq[g // 2, lax.rem(g, 2), s * block : (s + 1) * block, :] = jnp.broadcast_to(
                total, (block, HD)
            )
        scaled[pl.ds(pl.multiple_of(g * here, here), here), :] = jnp.dot(
            order, jnp.concatenate(parts, axis=0), preferred_element_type=jnp.float32
        ).astype(jnp.bfloat16)

    pl.semaphore_wait(barrier, len(peers))
    send_sq().start()

    def pass_on(n):
        send_pair(n).wait_recv()
        for d in range(pairs - 1):
            there = lax.rem(pair + d + 1, pairs)
            both = (prod[n, there, side] + from_other[n, there]).astype(jnp.bfloat16)
            for f in range(HALVES):
                to_along[n, f, d] = both[f * half : (f + 1) * half]
            send_along(n, 0, d).start()

    @pl.loop(0, chunks)
    def _(n):
        in_copy(n).wait()
        product = jnp.dot(scaled[...], weights[n], preferred_element_type=jnp.float32)
        prod[n] = product.reshape(pairs, 2, here, cw)
        send_pair(n).start()

        @pl.when(n == 0)
        def _():
            send_sq().wait()
            for d in range(pairs - 1):
                there = lax.rem(pair + d + 1, pairs)
                sq_to[d] = sq[there, side] + sq_other[there]
                send_sq_along(d).start()

        @pl.when(n >= LAG)
        def _():
            pass_on(n - LAG)

    @pl.loop(chunks - LAG, chunks)
    def _(n):
        pass_on(n)

    @pl.loop(0, chunks)
    def _(n):
        for f in range(1, HALVES):
            for d in range(pairs - 1):
                send_along(n, f, d).start()

    @pl.loop(0, out_blocks)
    def _(n):
        for p in range(pieces):
            out_copy(n, p).start()

    squares = sq[pair, side] + sq_other[pair]
    arrived(sq_along, sqa_recv)
    for d in range(pairs - 1):
        squares = squares + sq_along[d]
    factor = lax.rsqrt(squares / width + norm_eps)
    for f in range(HALVES):
        for z in range(inner):
            for s in range(STEPS):
                target = f * half + z * tile + s * half_rows
                row = s * block + z * rows + f * half_rows
                sq[0, 0, target : target + half_rows, :] = factor[row : row + half_rows]

    index = lax.rem(lax.broadcasted_iota(jnp.int32, (SUB, HD), 0), tile)
    lane = lax.broadcasted_iota(jnp.int32, (SUB, HD), 1)
    cosines, sines = [], []
    for f in range(HALVES):
        position = jnp.zeros((SUB, HD), jnp.float32)
        for s in range(STEPS):
            for i in range(half_rows):
                position = jnp.where(
                    index == s * half_rows + i,
                    (lengths[f * half_rows + i] + s).astype(jnp.float32),
                    position,
                )
        angle = position * freq[...]
        cosines.append(jnp.cos(angle))
        sines.append(jnp.where(lane < HD // 2, -jnp.sin(angle), jnp.sin(angle)))

    def settle(n, f):
        arrived(from_along.at[n, f], along_recv.at[n, f])
        span = slice(f * half, (f + 1) * half)
        for h in range(chunk_heads):
            columns = slice(h * HD, (h + 1) * HD)
            total = prod[n, pair, side, span, columns] + from_other[n, pair, span, columns]
            for d in range(pairs - 1):
                total = total + from_along[n, f, d, :, columns].astype(jnp.float32)
            total = total * sq[0, 0, span, :]
            for z in range(inner):
                mixed[z, h * tile : (h + 1) * tile, :] = total[z * tile : (z + 1) * tile]
        for z in range(inner):
            to_across[n, f, z] = (
                mixed[z].reshape(chunk_heads // per_tile, SUB, HD).astype(jnp.bfloat16)
            )
        for d in range(inner - 1):
            send_across(n, f, d).start()
        keep_own(n, f).start()

    early = chunks // 2

    @pl.loop(0, chunks)
    def _(n):
        settle(n, 0)

    @pl.loop(0, early)
    def _(n):
        settle(n, 1)

    upper = lax.broadcasted_iota(jnp.int32, (SUB, HD), 0) < tile
    queries = size // per_tile
    kv_heads = inner * groups
    columns = kv_heads * STEPS * size
    slot = lax.broadcasted_iota(jnp.int32, (slots + EXTRA, columns), 0)
    column = lax.broadcasted_iota(jnp.int32, (1, columns), 1)
    newest = jnp.where(lax.rem(column, STEPS * size) >= size, slots + 1, slots)

    def forward(f, d):
        for e in range(pairs - 1):
            gather(f, d, e).start()

    def forward_all(f):
        for d in range(1, inner):
            send_rows(f, d - 1).wait_recv()
            forward(f, d)
        share(f, 0).start()

    fresh[...] = jnp.zeros_like(fresh)

    @pl.loop(0, half_rows)
    def _(i):
        spread[i] = jnp.zeros(spread.shape[1:], jnp.bfloat16)

    for copy in kv_copies:
        copy.wait()

    for f in range(HALVES):

        @pl.loop(0, chunks)
        def _(n):
            if f > 0:

                @pl.when(n >= early)
                def _():
                    settle(n, f)

        if f > 0:
            forward_all(f - 1)
        arrived(joined.at[0, :, f], own_sem.at[f])
        arrived(joined.at[pl.ds(0, inner - 1), :, f], across_recv.at[f])

        @pl.loop(0, inner)
        def _(y):
            here_now = joined[y, :, f].reshape(groups * per * tile // SUB, SUB, HD)
            for j in range(groups):
                k = y * groups + j
                turn = here_now[j * per * tile // SUB : (j + 1) * per * tile // SUB]
                turn = turn.astype(jnp.float32)
                turned_now = turn * cosines[f][None] + pltpu.roll(turn, HD // 2, 2) * sines[f][None]
                turned_now = turned_now.astype(jnp.bfloat16).astype(jnp.float32)
                turned[j, : size * tile] = turned_now[:queries].reshape(size * tile, HD)
                turned[j, size * tile :] = jnp.where(upper, turned_now[queries], turn[queries])
                place = pl.ds(pl.multiple_of(k * HD, HD), HD)
                band = pl.ds(pl.multiple_of(k * STEPS * size, STEPS * size), STEPS * size)
                for i in range(half_rows):
                    query = jnp.concatenate(
                        [
                            turned[j, pl.ds(s * half_rows + i, size, stride=tile), :]
                            for s in range(STEPS)
                        ],
                        axis=0,
                    )
                    spread[i, band, place] = query.astype(jnp.bfloat16)
                    for s in range(STEPS):
                        for c in range(2):
                            row = (size + c) * tile + s * half_rows + i
                            fresh[i, c, s : s + 1, place] = turned[j, row : row + 1, :]

        for i in range(half_rows):
            row = f * half_rows + i
            k_here[row, slots:, :] = fresh[i, 0].astype(jnp.bfloat16)
            v_here[row, slots:, :] = fresh[i, 1].astype(jnp.bfloat16)
            scores = (
                lax.dot_general(
                    k_here[row],
                    spread[i],
                    (((1,), (1,)), ((), ())),
                    preferred_element_type=jnp.float32,
                )
                * scale
            )
            valid = (slot < lengths[row]) | ((slot >= slots) & (slot <= newest))
            scores = jnp.where(valid, scores, -jnp.inf)
            soft = jnp.exp(scores - jnp.max(scores, axis=0, keepdims=True))
            total = jnp.sum(soft, axis=0, keepdims=True)
            total = jnp.broadcast_to(total, (SUB, columns)).T
            soft = soft.astype(jnp.bfloat16).T
            for k in range(kv_heads):
                band = slice(k * STEPS * size, (k + 1) * STEPS * size)
                blend = jnp.dot(
                    soft[band],
                    v_here[row, :, k * HD : (k + 1) * HD],
                    preferred_element_type=jnp.float32,
                )
                blend = blend / total[band, 0:1]
                for s in range(STEPS):
                    mix[k, pl.ds(s * half_rows + i, size, stride=tile), :] = blend[
                        s * size : (s + 1) * size
                    ]

        for d in range(inner):
            there = lax.rem(gy + d + 1, inner)
            for j in range(groups):
                to_rows[f, d, j] = (
                    mix[there * groups + j].reshape(queries, SUB, HD).astype(jnp.bfloat16)
                )
            if d < inner - 1:
                send_rows(f, d).start()
        keep_rows(f).start()
        keep_rows(f).wait()
        forward(f, 0)

    heads_piece = depth // HD
    span = inner * tile

    def pass_side(f):
        for e in range(pairs - 1):
            arrived(held.at[f, 0], gather_recv.at[f, e])
            share(f, e + 1).start()

    def bring(f):
        for e in range(pairs):
            share(f, e).wait_recv()

        @pl.loop(0, outer)
        def _(g):
            place = pl.ds(pl.multiple_of(g * span, span), span)
            for j in range(groups):
                for q in range(queries):
                    both = held[f, g, :, j, q].astype(jnp.float32)
                    for t in range(per_tile):
                        for z in range(inner):
                            parted[q, t, z * tile : (z + 1) * tile, :] = both[
                                z, t * tile : (t + 1) * tile
                            ]
                    for t in range(per_tile):
                        head = j * size + q * per_tile + t
                        column = (head % heads_piece) * HD
                        flat[f, head // heads_piece, place, column : column + HD] = parted[
                            q, t
                        ].astype(jnp.bfloat16)

    for f in range(HALVES):
        if f < HALVES - 1:
            pass_side(f)
        if f == max(HALVES - 2, 0):
            forward_all(HALVES - 1)
        if f == HALVES - 1:
            pass_side(f)
        bring(f)

        def multiply(n):
            total = None
            if f == 0:
                out_ready(n).wait()
            for p in range(pieces):
                product = jnp.dot(
                    flat[f, p], weights[n * pieces + p], preferred_element_type=jnp.float32
                )
                total = product if total is None else total + product
            own[f, n] = total.reshape(inner, part, cw)

        if relays[f]:

            @pl.loop(0, relays[f])
            def _(n):
                multiply(n)
                k = relay_index(f, n)
                wide_near[k] = own[f, n, near_far]
                send_wide(k).start()
                to_near[k] = own[f, n, near].astype(jnp.bfloat16)
                send_near(k).start()

        @pl.loop(relays[f], out_blocks)
        def _(n):
            multiply(n)
            for d in range(inner - 1):
                to_sum[f, n, d] = own[f, n, lax.rem(gy + d + 1, inner)].astype(jnp.bfloat16)
                send_sum(f, n, d).start()

        if relays[f]:

            @pl.loop(0, relays[f])
            def _(n):
                k = relay_index(f, n)
                send_wide(k).wait_recv()
                to_far[k] = (own[f, n, far] + wide_from[k]).astype(jnp.bfloat16)
                send_far(k).start()

    for f in range(HALVES):

        def settle_sum(n, terms):
            for c in range(cw // HD):
                columns = slice(c * HD, (c + 1) * HD)
                total = own[f, n, gy, :, columns]
                for term in terms:
                    total = total + term[:, columns].astype(jnp.float32)
                place = pl.ds(pl.multiple_of(n * cw + c * HD, HD), HD)
                for q in range(part // tile):
                    for s in range(STEPS):
                        start = q * tile + s * half_rows
                        target = q * rows + f * half_rows
                        piece[s, target : target + half_rows, place] = total[
                            start : start + half_rows
                        ]
                if f == HALVES - 1:
                    for s in range(STEPS):
                        result[s, :, place] = piece[s, :, place].astype(jnp.bfloat16)

        if relays[f]:

            @pl.loop(0, relays[f])
            def _(n):
                k = relay_index(f, n)
                send_near(k).wait_recv()
                send_far(k).wait_recv()
                settle_sum(n, [from_near.at[k], from_far.at[k]])

        @pl.loop(relays[f], out_blocks)
        def _(n):
            arrived(from_sum.at[f, n], sum_recv.at[f, n])
            settle_sum(n, [from_sum.at[f, n, d] for d in range(inner - 1)])

    arrived(prod.at[:, :, 0], pair_send)
    arrived(sq_to, sqa_send)
    for f in range(HALVES):
        arrived(to_along.at[:, f], along_send.at[f])
        arrived(to_across.at[:, f, pl.ds(0, inner - 1)], across_send.at[f])
        arrived(to_rows.at[f, pl.ds(0, inner - 1)], rows_send.at[f])
        arrived(held.at[f, pl.ds(0, pairs - 1)], gather_send.at[f])
        arrived(held.at[f, pl.ds(0, pairs)], share_send.at[f])
        arrived(to_sum.at[f, pl.ds(relays[f], out_blocks - relays[f])], sum_send.at[f])
    if sum(relays):
        arrived(to_near, near_send)
        arrived(wide_near, wide_send)
        arrived(to_far, far_send)


def body(x_first, x_second, norm_gain, w_qkv, w_out, cache_keys, cache_values, lengths):
    outer, inner = lax.axis_size("gx"), lax.axis_size("gy")
    rows, slots, kv_width = cache_keys.shape
    depth, in_columns = w_qkv.shape
    out_depth, out_columns = w_out.shape
    width = depth * outer
    heads = in_columns // HD
    groups = kv_width // HD // inner
    size = heads // groups - 2
    chunk_heads = 4 if in_columns % (4 * HD) == 0 and out_columns % (4 * HD) == 0 else 2
    chunks = heads // chunk_heads
    cw = chunk_heads * HD
    pairs = outer // 2
    here = STEPS * inner * rows
    tile = STEPS * rows // HALVES
    queries = size * tile // SUB
    total = outer * here // HALVES
    part = total // inner
    out_blocks = out_columns // cw
    pieces = out_depth // depth
    relayed = max(1, sum(relays_of(inner, out_blocks)))
    dims = (outer, inner, rows, width, groups, size, chunk_heads, chunks)

    half = HD // 2
    freq = rotary_base ** (-(np.arange(half, dtype=np.float64) * 2.0 / HD))
    freq = jnp.asarray(np.tile(freq, 2)[None], jnp.float32)

    dma = pltpu.SemaphoreType.DMA
    vmem = pl.BlockSpec(memory_space=pltpu.VMEM)
    away = pl.BlockSpec(memory_space=pl.ANY)
    f32, b16 = jnp.float32, jnp.bfloat16
    result = pl.pallas_call(
        functools.partial(block_kernel, dims),
        in_specs=[
            pl.BlockSpec(memory_space=pltpu.SMEM), away, away, vmem, vmem, away, away, away, away,
        ],
        out_specs=vmem,
        out_shape=jax.ShapeDtypeStruct((STEPS, HALVES * part // STEPS, out_columns), b16),
        scratch_shapes=[
            pltpu.VMEM((STEPS, outer * inner * rows, depth), b16),
            pltpu.VMEM((rows, slots + EXTRA, kv_width), b16),
            pltpu.VMEM((rows, slots + EXTRA, kv_width), b16),
            pltpu.VMEM((max(in_columns // cw, out_blocks * pieces), depth, cw), b16),
            pltpu.VMEM((outer * here, depth), b16),
            pltpu.VMEM((chunks, pairs, 2, here, cw), f32),
            pltpu.VMEM((chunks, pairs, here, cw), f32),
            pltpu.VMEM((chunks, HALVES, pairs - 1, here // HALVES, cw), b16),
            pltpu.VMEM((chunks, HALVES, pairs - 1, here // HALVES, cw), b16),
            pltpu.VMEM((pairs, 2, here, HD), f32),
            pltpu.VMEM((pairs, here, HD), f32),
            pltpu.VMEM((pairs - 1, here, HD), f32),
            pltpu.VMEM((pairs - 1, here, HD), f32),
            pltpu.VMEM((inner, chunk_heads * tile, HD), f32),
            pltpu.VMEM((chunks, HALVES, inner, chunk_heads * tile // SUB, SUB, HD), b16),
            pltpu.VMEM((inner, chunks, HALVES, chunk_heads * tile // SUB, SUB, HD), b16),
            pltpu.VMEM((groups, (size + 2) * tile, HD), f32),
            pltpu.VMEM((rows // HALVES, kv_width // HD * STEPS * size, kv_width), b16),
            pltpu.VMEM((rows // HALVES, 2, EXTRA, kv_width), f32),
            pltpu.VMEM((kv_width // HD, size * tile, HD), f32),
            pltpu.VMEM((HALVES, inner, groups, queries, SUB, HD), b16),
            pltpu.VMEM((HALVES, outer, inner, groups, queries, SUB, HD), b16),
            pltpu.VMEM((queries, SUB // tile, inner * tile, HD), f32),
            pltpu.VMEM((HALVES, pieces, total, depth), b16),
            pltpu.VMEM((HALVES, out_blocks, inner, part, cw), f32),
            pltpu.VMEM((HALVES, out_blocks, inner - 1, part, cw), b16),
            pltpu.VMEM((HALVES, out_blocks, inner - 1, part, cw), b16),
            pltpu.VMEM((STEPS, HALVES * part // STEPS, out_columns), f32),
            pltpu.VMEM((relayed, part, cw), b16),
            pltpu.VMEM((relayed, part, cw), b16),
            pltpu.VMEM((relayed, part, cw), f32),
            pltpu.VMEM((relayed, part, cw), f32),
            pltpu.VMEM((relayed, part, cw), b16),
            pltpu.VMEM((relayed, part, cw), b16),
            dma((STEPS,)), dma((2,)), dma((chunks,)), dma((out_blocks,)),
            dma, dma((chunks,)),
            dma((HALVES,)), dma((chunks, HALVES)),
            dma((HALVES,)), dma((HALVES,)),
            dma, dma, dma, dma, dma((HALVES,)),
            dma((HALVES,)), dma((HALVES, inner - 1)), dma((HALVES,)),
            dma((HALVES,)), dma((HALVES, pairs - 1)),
            dma((HALVES,)), dma((HALVES, pairs)),
            dma((HALVES,)), dma((HALVES, out_blocks)),
            dma, dma((relayed,)), dma, dma((relayed,)), dma, dma((relayed,)),
        ],
        compiler_params=pltpu.CompilerParams(
            collective_id=0, has_side_effects=True, vmem_limit_bytes=VMEM_LIMIT
        ),
        name="decode_block",
    )(lengths, x_first, x_second, norm_gain, freq, w_qkv, w_out, cache_keys, cache_values)
    return result[0], result[1]


def solution(mesh):
    in_specs = (
        P(None, "gx"),
        P(None, "gx"),
        P("gx"),
        P("gx", "gy"),
        P("gy", "gx"),
        P(("gx", "gy"), None, None),
        P(("gx", "gy"), None, None),
        P(("gx", "gy")),
    )
    out_specs = (P("gy", "gx"), P("gy", "gx"))
    return jax.shard_map(body, mesh=mesh, in_specs=in_specs, out_specs=out_specs, check_vma=False)
```

```python
import functools
import math

import jax
import jax.numpy as jnp
import numpy as np
from jax import lax
from jax.experimental import pallas as pl
from jax.experimental.pallas import tpu as pltpu
from jax.sharding import PartitionSpec as P

HD = 128
norm_eps = 1e-05
rotary_base = 500000.0
STEPS = 2
HALVES = 2
SUB = 8
EXTRA = 16
LAG = 2
RELAYS = (2, 2)
VMEM_LIMIT = 62 * 1024 * 1024
MESH = pl.DeviceIdType.MESH


def remote(src, dst, send, recv, device):
    return pltpu.make_async_remote_copy(
        src_ref=src, dst_ref=dst, send_sem=send, recv_sem=recv,
        device_id=device, device_id_type=MESH,
    )


def relays_of(inner, out_blocks):
    return RELAYS if inner == 4 and out_blocks > max(RELAYS) else (0,) * HALVES


def block_kernel(
    dims, lengths, x_first, x_second, gain, freq, w_in, w_out, keys, values, result,
    x_here, k_here, v_here, weights, scaled, prod, from_other, to_along, from_along,
    sq, sq_other, sq_to, sq_along, mixed, to_across, joined,
    turned, spread, fresh, mix, to_rows, held, parted, flat, own, to_sum, from_sum, piece,
    to_near, from_near, wide_near, wide_from, to_far, from_far,
    x_sem, kv_sem, in_sem, out_sem, pair_send, pair_recv, along_send, along_recv,
    across_send, across_recv, sq_send, sq_recv, sqa_send, sqa_recv, own_sem,
    rows_send, rows_recv, keep_sem, gather_send, gather_recv, share_send, share_recv,
    sum_send, sum_recv, near_send, near_recv, wide_send, wide_recv, far_send, far_recv,
):
    outer, inner, rows, width, groups, size, chunk_heads, chunks = dims
    gx, gy = lax.axis_index("gx"), lax.axis_index("gy")
    pairs = outer // 2
    pair, side = gx // 2, lax.rem(gx, 2)
    other = (gx + 1 - 2 * side, gy)
    along = [(2 * lax.rem(pair + d, pairs) + side, gy) for d in range(1, pairs)]
    across = [(gx, lax.rem(gy + d, inner)) for d in range(1, inner)]
    cw = chunk_heads * HD
    block = inner * rows
    here = STEPS * block
    half_rows = rows // HALVES
    tile = STEPS * half_rows
    per_tile = SUB // tile
    per = size + 2
    slots = k_here.shape[1] - EXTRA
    half = here // HALVES
    depth = scaled.shape[1]
    out_blocks = own.shape[1]
    pieces = flat.shape[1]
    part = own.shape[3]
    scale = 1.0 / math.sqrt(HD)

    x_copies = [
        pltpu.make_async_copy(x, x_here.at[s], x_sem.at[s])
        for s, x in enumerate((x_first, x_second))
    ]

    def in_copy(b):
        return pltpu.make_async_copy(
            w_in.at[:, pl.ds(pl.multiple_of(b * cw, cw), cw)], weights.at[b], in_sem.at[b]
        )

    def out_copy(n, p):
        return pltpu.make_async_copy(
            w_out.at[
                pl.ds(p * depth, depth), pl.ds(pl.multiple_of(n * cw, cw), cw)
            ],
            weights.at[n * pieces + p],
            out_sem.at[n],
        )

    def out_ready(n):
        ref = weights.at[pl.ds(n * pieces, pieces)]
        return pltpu.make_async_copy(ref, ref, out_sem.at[n])

    kv_copies = [
        pltpu.make_async_copy(keys, k_here.at[:, pl.ds(0, slots)], kv_sem.at[0]),
        pltpu.make_async_copy(values, v_here.at[:, pl.ds(0, slots)], kv_sem.at[1]),
    ]

    def send_sq():
        return remote(sq.at[:, 1 - side], sq_other, sq_send, sq_recv, other)

    def send_sq_along(d):
        return remote(sq_to.at[d], sq_along.at[d], sqa_send, sqa_recv, along[d])

    def send_pair(n):
        return remote(
            prod.at[n, :, 1 - side], from_other.at[n], pair_send, pair_recv.at[n], other
        )

    def send_along(n, f, d):
        return remote(
            to_along.at[n, f, d], from_along.at[n, f, d],
            along_send.at[f], along_recv.at[n, f], along[d],
        )

    def send_across(n, f, d):
        return remote(
            to_across.at[n, f, lax.rem(gy + d + 1, inner)], joined.at[gy, n, f],
            across_send.at[f], across_recv.at[f], across[d],
        )

    def keep_own(n, f):
        return pltpu.make_async_copy(
            to_across.at[n, f, gy], joined.at[gy, n, f], own_sem.at[f]
        )

    def source(d):
        return lax.rem(gy + inner - d, inner)

    def send_rows(f, d):
        return remote(
            to_rows.at[f, d], held.at[f, gx, gy], rows_send.at[f], rows_recv.at[f, d], across[d]
        )

    def keep_rows(f):
        return pltpu.make_async_copy(
            to_rows.at[f, inner - 1], held.at[f, gx, gy], keep_sem.at[f]
        )

    def gather(f, d, e):
        ref = held.at[f, gx, source(d)]
        return remote(ref, ref, gather_send.at[f], gather_recv.at[f, e], along[e])

    def share(f, e):
        ref = held.at[f, 2 * lax.rem(pair + pairs - e, pairs) + side]
        return remote(ref, ref, share_send.at[f], share_recv.at[f, e], other)

    def send_sum(f, n, d):
        return remote(
            to_sum.at[f, n, d], from_sum.at[f, n, d],
            sum_send.at[f], sum_recv.at[f, n], across[d],
        )

    relays = relays_of(inner, out_blocks)
    near = gy + 1 - 2 * lax.rem(gy, 2)
    near_far, far = lax.rem(near + 2, inner), lax.rem(gy + 2, inner)

    def relay_index(f, n):
        return sum(relays[:f]) + n

    def send_near(k):
        return remote(to_near.at[k], from_near.at[k], near_send, near_recv.at[k], (gx, near))

    def send_wide(k):
        return remote(wide_near.at[k], wide_from.at[k], wide_send, wide_recv.at[k], (gx, near))

    def send_far(k):
        return remote(to_far.at[k], from_far.at[k], far_send, far_recv.at[k], (gx, far))

    def arrived(ref, sem):
        pltpu.make_async_copy(ref, ref, sem).wait()

    for copy in x_copies:
        copy.start()

    @pl.loop(0, chunks)
    def _(b):
        in_copy(b).start()

    for copy in kv_copies:
        copy.start()

    barrier = pltpu.get_barrier_semaphore()
    peers = [other] + along + across
    for peer in peers:
        pl.semaphore_signal(barrier, inc=1, device_id=peer, device_id_type=MESH)

    to = lax.broadcasted_iota(jnp.int32, (here, here), 0)
    step = lax.rem(lax.div(to, half_rows), STEPS)
    member = lax.rem(lax.div(to, tile), inner)
    start = lax.div(to, half) * half_rows + lax.rem(to, half_rows)
    source_row = step * block + member * rows + start
    order = jnp.where(
        source_row == lax.broadcasted_iota(jnp.int32, (here, here), 1), 1.0, 0.0
    ).astype(jnp.bfloat16)
    wide_gain = gain[...].astype(jnp.float32).reshape(1, depth)
    for copy in x_copies:
        copy.wait()

    @pl.loop(0, outer)
    def _(g):
        parts = []
        for s in range(STEPS):
            wide = x_here[s, pl.ds(pl.multiple_of(g * block, block), block), :].astype(jnp.float32)
            parts.append((wide * wide_gain).astype(jnp.bfloat16))
            total = jnp.sum(wide * wide, axis=1, keepdims=True)
            sq[g // 2, lax.rem(g, 2), s * block : (s + 1) * block, :] = jnp.broadcast_to(
                total, (block, HD)
            )
        scaled[pl.ds(pl.multiple_of(g * here, here), here), :] = jnp.dot(
            order, jnp.concatenate(parts, axis=0), preferred_element_type=jnp.float32
        ).astype(jnp.bfloat16)

    pl.semaphore_wait(barrier, len(peers))
    send_sq().start()

    def pass_on(n):
        send_pair(n).wait_recv()
        for d in range(pairs - 1):
            there = lax.rem(pair + d + 1, pairs)
            both = (prod[n, there, side] + from_other[n, there]).astype(jnp.bfloat16)
            for f in range(HALVES):
                to_along[n, f, d] = both[f * half : (f + 1) * half]
            send_along(n, 0, d).start()

    @pl.loop(0, chunks)
    def _(n):
        in_copy(n).wait()
        product = jnp.dot(scaled[...], weights[n], preferred_element_type=jnp.float32)
        prod[n] = product.reshape(pairs, 2, here, cw)
        send_pair(n).start()

        @pl.when(n == 0)
        def _():
            send_sq().wait()
            for d in range(pairs - 1):
                there = lax.rem(pair + d + 1, pairs)
                sq_to[d] = sq[there, side] + sq_other[there]
                send_sq_along(d).start()

        @pl.when(n >= LAG)
        def _():
            pass_on(n - LAG)

    @pl.loop(chunks - LAG, chunks)
    def _(n):
        pass_on(n)

    @pl.loop(0, chunks)
    def _(n):
        for f in range(1, HALVES):
            for d in range(pairs - 1):
                send_along(n, f, d).start()

    @pl.loop(0, out_blocks)
    def _(n):
        for p in range(pieces):
            out_copy(n, p).start()

    squares = sq[pair, side] + sq_other[pair]
    arrived(sq_along, sqa_recv)
    for d in range(pairs - 1):
        squares = squares + sq_along[d]
    factor = lax.rsqrt(squares / width + norm_eps)
    for f in range(HALVES):
        for z in range(inner):
            for s in range(STEPS):
                target = f * half + z * tile + s * half_rows
                row = s * block + z * rows + f * half_rows
                sq[0, 0, target : target + half_rows, :] = factor[row : row + half_rows]

    index = lax.rem(lax.broadcasted_iota(jnp.int32, (SUB, HD), 0), tile)
    lane = lax.broadcasted_iota(jnp.int32, (SUB, HD), 1)
    cosines, sines = [], []
    for f in range(HALVES):
        position = jnp.zeros((SUB, HD), jnp.float32)
        for s in range(STEPS):
            for i in range(half_rows):
                position = jnp.where(
                    index == s * half_rows + i,
                    (lengths[f * half_rows + i] + s).astype(jnp.float32),
                    position,
                )
        angle = position * freq[...]
        cosines.append(jnp.cos(angle))
        sines.append(jnp.where(lane < HD // 2, -jnp.sin(angle), jnp.sin(angle)))

    def settle(n, f):
        arrived(from_along.at[n, f], along_recv.at[n, f])
        span = slice(f * half, (f + 1) * half)
        for h in range(chunk_heads):
            columns = slice(h * HD, (h + 1) * HD)
            total = prod[n, pair, side, span, columns] + from_other[n, pair, span, columns]
            for d in range(pairs - 1):
                total = total + from_along[n, f, d, :, columns].astype(jnp.float32)
            total = total * sq[0, 0, span, :]
            for z in range(inner):
                mixed[z, h * tile : (h + 1) * tile, :] = total[z * tile : (z + 1) * tile]
        for z in range(inner):
            to_across[n, f, z] = (
                mixed[z].reshape(chunk_heads // per_tile, SUB, HD).astype(jnp.bfloat16)
            )
        for d in range(inner - 1):
            send_across(n, f, d).start()
        keep_own(n, f).start()

    early = chunks // 2

    @pl.loop(0, chunks)
    def _(n):
        settle(n, 0)

    @pl.loop(0, early)
    def _(n):
        settle(n, 1)

    upper = lax.broadcasted_iota(jnp.int32, (SUB, HD), 0) < tile
    queries = size // per_tile
    kv_heads = inner * groups
    columns = kv_heads * STEPS * size
    slot = lax.broadcasted_iota(jnp.int32, (slots + EXTRA, columns), 0)
    column = lax.broadcasted_iota(jnp.int32, (1, columns), 1)
    newest = jnp.where(lax.rem(column, STEPS * size) >= size, slots + 1, slots)

    def forward(f, d):
        for e in range(pairs - 1):
            gather(f, d, e).start()

    def forward_all(f):
        for d in range(1, inner):
            send_rows(f, d - 1).wait_recv()
            forward(f, d)
        share(f, 0).start()

    fresh[...] = jnp.zeros_like(fresh)

    @pl.loop(0, half_rows)
    def _(i):
        spread[i] = jnp.zeros(spread.shape[1:], jnp.bfloat16)

    for copy in kv_copies:
        copy.wait()

    for f in range(HALVES):

        @pl.loop(0, chunks)
        def _(n):
            if f > 0:

                @pl.when(n >= early)
                def _():
                    settle(n, f)

        if f > 0:
            forward_all(f - 1)
        arrived(joined.at[0, :, f], own_sem.at[f])
        arrived(joined.at[pl.ds(0, inner - 1), :, f], across_recv.at[f])

        @pl.loop(0, inner)
        def _(y):
            here_now = joined[y, :, f].reshape(groups * per * tile // SUB, SUB, HD)
            for j in range(groups):
                k = y * groups + j
                turn = here_now[j * per * tile // SUB : (j + 1) * per * tile // SUB]
                turn = turn.astype(jnp.float32)
                turned_now = turn * cosines[f][None] + pltpu.roll(turn, HD // 2, 2) * sines[f][None]
                turned_now = turned_now.astype(jnp.bfloat16).astype(jnp.float32)
                turned[j, : size * tile] = turned_now[:queries].reshape(size * tile, HD)
                turned[j, size * tile :] = jnp.where(upper, turned_now[queries], turn[queries])
                place = pl.ds(pl.multiple_of(k * HD, HD), HD)
                band = pl.ds(pl.multiple_of(k * STEPS * size, STEPS * size), STEPS * size)
                for i in range(half_rows):
                    query = jnp.concatenate(
                        [
                            turned[j, pl.ds(s * half_rows + i, size, stride=tile), :]
                            for s in range(STEPS)
                        ],
                        axis=0,
                    )
                    spread[i, band, place] = query.astype(jnp.bfloat16)
                    for s in range(STEPS):
                        for c in range(2):
                            row = (size + c) * tile + s * half_rows + i
                            fresh[i, c, s : s + 1, place] = turned[j, row : row + 1, :]

        for i in range(half_rows):
            row = f * half_rows + i
            k_here[row, slots:, :] = fresh[i, 0].astype(jnp.bfloat16)
            v_here[row, slots:, :] = fresh[i, 1].astype(jnp.bfloat16)
            scores = (
                lax.dot_general(
                    k_here[row],
                    spread[i],
                    (((1,), (1,)), ((), ())),
                    preferred_element_type=jnp.float32,
                )
                * scale
            )
            valid = (slot < lengths[row]) | ((slot >= slots) & (slot <= newest))
            scores = jnp.where(valid, scores, -jnp.inf)
            soft = jnp.exp(scores - jnp.max(scores, axis=0, keepdims=True))
            total = jnp.sum(soft, axis=0, keepdims=True)
            total = jnp.broadcast_to(total, (SUB, columns)).T
            soft = soft.astype(jnp.bfloat16).T
            for k in range(kv_heads):
                band = slice(k * STEPS * size, (k + 1) * STEPS * size)
                blend = jnp.dot(
                    soft[band],
                    v_here[row, :, k * HD : (k + 1) * HD],
                    preferred_element_type=jnp.float32,
                )
                blend = blend / total[band, 0:1]
                for s in range(STEPS):
                    mix[k, pl.ds(s * half_rows + i, size, stride=tile), :] = blend[
                        s * size : (s + 1) * size
                    ]

        for d in range(inner):
            there = lax.rem(gy + d + 1, inner)
            for j in range(groups):
                to_rows[f, d, j] = (
                    mix[there * groups + j].reshape(queries, SUB, HD).astype(jnp.bfloat16)
                )
            if d < inner - 1:
                send_rows(f, d).start()
        keep_rows(f).start()
        keep_rows(f).wait()
        forward(f, 0)

    heads_piece = depth // HD
    span = inner * tile

    def pass_side(f):
        for e in range(pairs - 1):
            arrived(held.at[f, 0], gather_recv.at[f, e])
            share(f, e + 1).start()

    def bring(f):
        fill(f, side)
        for e in range(pairs):
            share(f, e).wait_recv()
        fill(f, 1 - side)

    def fill(f, which):
        @pl.loop(0, pairs)
        def _(c):
            g = 2 * c + which
            place = pl.ds(pl.multiple_of(g * span, span), span)
            for j in range(groups):
                for q in range(queries):
                    both = held[f, g, :, j, q].astype(jnp.float32)
                    for t in range(per_tile):
                        for z in range(inner):
                            parted[q, t, z * tile : (z + 1) * tile, :] = both[
                                z, t * tile : (t + 1) * tile
                            ]
                    for t in range(per_tile):
                        head = j * size + q * per_tile + t
                        column = (head % heads_piece) * HD
                        flat[f, head // heads_piece, place, column : column + HD] = parted[
                            q, t
                        ].astype(jnp.bfloat16)

    def relay_on(f):
        if relays[f]:

            @pl.loop(0, relays[f])
            def _(n):
                k = relay_index(f, n)
                send_wide(k).wait_recv()
                to_far[k] = (own[f, n, far] + wide_from[k]).astype(jnp.bfloat16)
                send_far(k).start()

    for f in range(HALVES):
        if f < HALVES - 1:
            pass_side(f)
        if f == max(HALVES - 2, 0):
            forward_all(HALVES - 1)
        if f == HALVES - 1:
            pass_side(f)
            relay_on(f - 1)
        bring(f)

        def multiply(n):
            total = None
            if f == 0:
                out_ready(n).wait()
            for p in range(pieces):
                product = jnp.dot(
                    flat[f, p], weights[n * pieces + p], preferred_element_type=jnp.float32
                )
                total = product if total is None else total + product
            own[f, n] = total.reshape(inner, part, cw)

        if relays[f]:

            @pl.loop(0, relays[f])
            def _(n):
                multiply(n)
                k = relay_index(f, n)
                wide_near[k] = own[f, n, near_far]
                send_wide(k).start()
                to_near[k] = own[f, n, near].astype(jnp.bfloat16)
                send_near(k).start()

        @pl.loop(relays[f], out_blocks)
        def _(n):
            multiply(n)
            for d in range(inner - 1):
                to_sum[f, n, d] = own[f, n, lax.rem(gy + d + 1, inner)].astype(jnp.bfloat16)
                send_sum(f, n, d).start()

        if f == HALVES - 1:
            relay_on(f)

    for f in range(HALVES):

        def settle_sum(n, terms):
            for c in range(cw // HD):
                columns = slice(c * HD, (c + 1) * HD)
                total = own[f, n, gy, :, columns]
                for term in terms:
                    total = total + term[:, columns].astype(jnp.float32)
                place = pl.ds(pl.multiple_of(n * cw + c * HD, HD), HD)
                for q in range(part // tile):
                    for s in range(STEPS):
                        start = q * tile + s * half_rows
                        target = q * rows + f * half_rows
                        piece[s, target : target + half_rows, place] = total[
                            start : start + half_rows
                        ]
                if f == HALVES - 1:
                    for s in range(STEPS):
                        result[s, :, place] = piece[s, :, place].astype(jnp.bfloat16)

        if relays[f]:

            @pl.loop(0, relays[f])
            def _(n):
                k = relay_index(f, n)
                send_near(k).wait_recv()
                send_far(k).wait_recv()
                settle_sum(n, [from_near.at[k], from_far.at[k]])

        @pl.loop(relays[f], out_blocks)
        def _(n):
            arrived(from_sum.at[f, n], sum_recv.at[f, n])
            settle_sum(n, [from_sum.at[f, n, d] for d in range(inner - 1)])

    arrived(prod.at[:, :, 0], pair_send)
    arrived(sq_to, sqa_send)
    for f in range(HALVES):
        arrived(to_along.at[:, f], along_send.at[f])
        arrived(to_across.at[:, f, pl.ds(0, inner - 1)], across_send.at[f])
        arrived(to_rows.at[f, pl.ds(0, inner - 1)], rows_send.at[f])
        arrived(held.at[f, pl.ds(0, pairs - 1)], gather_send.at[f])
        arrived(held.at[f, pl.ds(0, pairs)], share_send.at[f])
        arrived(to_sum.at[f, pl.ds(relays[f], out_blocks - relays[f])], sum_send.at[f])
    if sum(relays):
        arrived(to_near, near_send)
        arrived(wide_near, wide_send)
        arrived(to_far, far_send)


def body(x_first, x_second, norm_gain, w_qkv, w_out, cache_keys, cache_values, lengths):
    outer, inner = lax.axis_size("gx"), lax.axis_size("gy")
    rows, slots, kv_width = cache_keys.shape
    depth, in_columns = w_qkv.shape
    out_depth, out_columns = w_out.shape
    width = depth * outer
    heads = in_columns // HD
    groups = kv_width // HD // inner
    size = heads // groups - 2
    chunk_heads = 4 if in_columns % (4 * HD) == 0 and out_columns % (4 * HD) == 0 else 2
    chunks = heads // chunk_heads
    cw = chunk_heads * HD
    pairs = outer // 2
    here = STEPS * inner * rows
    tile = STEPS * rows // HALVES
    queries = size * tile // SUB
    total = outer * here // HALVES
    part = total // inner
    out_blocks = out_columns // cw
    pieces = out_depth // depth
    relayed = max(1, sum(relays_of(inner, out_blocks)))
    dims = (outer, inner, rows, width, groups, size, chunk_heads, chunks)

    half = HD // 2
    freq = rotary_base ** (-(np.arange(half, dtype=np.float64) * 2.0 / HD))
    freq = jnp.asarray(np.tile(freq, 2)[None], jnp.float32)

    dma = pltpu.SemaphoreType.DMA
    vmem = pl.BlockSpec(memory_space=pltpu.VMEM)
    away = pl.BlockSpec(memory_space=pl.ANY)
    f32, b16 = jnp.float32, jnp.bfloat16
    result = pl.pallas_call(
        functools.partial(block_kernel, dims),
        in_specs=[
            pl.BlockSpec(memory_space=pltpu.SMEM), away, away, vmem, vmem, away, away, away, away,
        ],
        out_specs=vmem,
        out_shape=pltpu.VMEM((STEPS, HALVES * part // STEPS, out_columns), b16),
        scratch_shapes=[
            pltpu.VMEM((STEPS, outer * inner * rows, depth), b16),
            pltpu.VMEM((rows, slots + EXTRA, kv_width), b16),
            pltpu.VMEM((rows, slots + EXTRA, kv_width), b16),
            pltpu.VMEM((max(in_columns // cw, out_blocks * pieces), depth, cw), b16),
            pltpu.VMEM((outer * here, depth), b16),
            pltpu.VMEM((chunks, pairs, 2, here, cw), f32),
            pltpu.VMEM((chunks, pairs, here, cw), f32),
            pltpu.VMEM((chunks, HALVES, pairs - 1, here // HALVES, cw), b16),
            pltpu.VMEM((chunks, HALVES, pairs - 1, here // HALVES, cw), b16),
            pltpu.VMEM((pairs, 2, here, HD), f32),
            pltpu.VMEM((pairs, here, HD), f32),
            pltpu.VMEM((pairs - 1, here, HD), f32),
            pltpu.VMEM((pairs - 1, here, HD), f32),
            pltpu.VMEM((inner, chunk_heads * tile, HD), f32),
            pltpu.VMEM((chunks, HALVES, inner, chunk_heads * tile // SUB, SUB, HD), b16),
            pltpu.VMEM((inner, chunks, HALVES, chunk_heads * tile // SUB, SUB, HD), b16),
            pltpu.VMEM((groups, (size + 2) * tile, HD), f32),
            pltpu.VMEM((rows // HALVES, kv_width // HD * STEPS * size, kv_width), b16),
            pltpu.VMEM((rows // HALVES, 2, EXTRA, kv_width), f32),
            pltpu.VMEM((kv_width // HD, size * tile, HD), f32),
            pltpu.VMEM((HALVES, inner, groups, queries, SUB, HD), b16),
            pltpu.VMEM((HALVES, outer, inner, groups, queries, SUB, HD), b16),
            pltpu.VMEM((queries, SUB // tile, inner * tile, HD), f32),
            pltpu.VMEM((HALVES, pieces, total, depth), b16),
            pltpu.VMEM((HALVES, out_blocks, inner, part, cw), f32),
            pltpu.VMEM((HALVES, out_blocks, inner - 1, part, cw), b16),
            pltpu.VMEM((HALVES, out_blocks, inner - 1, part, cw), b16),
            pltpu.VMEM((STEPS, HALVES * part // STEPS, out_columns), f32),
            pltpu.VMEM((relayed, part, cw), b16),
            pltpu.VMEM((relayed, part, cw), b16),
            pltpu.VMEM((relayed, part, cw), f32),
            pltpu.VMEM((relayed, part, cw), f32),
            pltpu.VMEM((relayed, part, cw), b16),
            pltpu.VMEM((relayed, part, cw), b16),
            dma((STEPS,)), dma((2,)), dma((chunks,)), dma((out_blocks,)),
            dma, dma((chunks,)),
            dma((HALVES,)), dma((chunks, HALVES)),
            dma((HALVES,)), dma((HALVES,)),
            dma, dma, dma, dma, dma((HALVES,)),
            dma((HALVES,)), dma((HALVES, inner - 1)), dma((HALVES,)),
            dma((HALVES,)), dma((HALVES, pairs - 1)),
            dma((HALVES,)), dma((HALVES, pairs)),
            dma((HALVES,)), dma((HALVES, out_blocks)),
            dma, dma((relayed,)), dma, dma((relayed,)), dma, dma((relayed,)),
        ],
        compiler_params=pltpu.CompilerParams(
            collective_id=0, has_side_effects=True, vmem_limit_bytes=VMEM_LIMIT
        ),
        name="decode_block",
    )(lengths, x_first, x_second, norm_gain, freq, w_qkv, w_out, cache_keys, cache_values)
    return result[0], result[1]


def solution(mesh):
    in_specs = (
        P(None, "gx"),
        P(None, "gx"),
        P("gx"),
        P("gx", "gy"),
        P("gy", "gx"),
        P(("gx", "gy"), None, None),
        P(("gx", "gy"), None, None),
        P(("gx", "gy")),
    )
    out_specs = (P("gy", "gx"), P("gy", "gx"))
    return jax.shard_map(body, mesh=mesh, in_specs=in_specs, out_specs=out_specs, check_vma=False)
```

```python
import functools
import math

import jax
import jax.numpy as jnp
import numpy as np
from jax import lax
from jax.experimental import pallas as pl
from jax.experimental.pallas import tpu as pltpu
from jax.sharding import PartitionSpec as P

HD = 128
norm_eps = 1e-05
rotary_base = 500000.0
STEPS = 2
HALVES = 2
SUB = 8
EXTRA = 16
LAG = 2
RELAYS = (2, 2)
VMEM_LIMIT = 62 * 1024 * 1024
MESH = pl.DeviceIdType.MESH


def remote(src, dst, send, recv, device):
    return pltpu.make_async_remote_copy(
        src_ref=src, dst_ref=dst, send_sem=send, recv_sem=recv,
        device_id=device, device_id_type=MESH,
    )


def relays_of(inner, out_blocks):
    return RELAYS if inner == 4 and out_blocks > max(RELAYS) else (0,) * HALVES


def block_kernel(
    dims, lengths, x_first, x_second, gain, freq, w_in, w_out, keys, values, result,
    x_here, k_here, v_here, weights, scaled, prod, from_other, to_along, from_along,
    sq, sq_other, sq_to, sq_along, mixed, to_across, joined,
    turned, spread, fresh, mix, to_rows, held, parted, flat, own, to_sum, from_sum, piece,
    to_near, from_near, wide_near, wide_from, to_far, from_far,
    x_sem, kv_sem, in_sem, out_sem, pair_send, pair_recv, along_send, along_recv,
    across_send, across_recv, sq_send, sq_recv, sqa_send, sqa_recv, own_sem,
    rows_send, rows_recv, keep_sem, gather_send, gather_recv, share_send, share_recv,
    sum_send, sum_recv, near_send, near_recv, wide_send, wide_recv, far_send, far_recv,
):
    outer, inner, rows, width, groups, size, chunk_heads, chunks = dims
    gx, gy = lax.axis_index("gx"), lax.axis_index("gy")
    pairs = outer // 2
    pair, side = gx // 2, lax.rem(gx, 2)
    other = (gx + 1 - 2 * side, gy)
    along = [(2 * lax.rem(pair + d, pairs) + side, gy) for d in range(1, pairs)]
    across = [(gx, lax.rem(gy + d, inner)) for d in range(1, inner)]
    cw = chunk_heads * HD
    block = inner * rows
    here = STEPS * block
    half_rows = rows // HALVES
    tile = STEPS * half_rows
    per_tile = SUB // tile
    per = size + 2
    slots = k_here.shape[1] - EXTRA
    half = here // HALVES
    depth = scaled.shape[1]
    out_blocks = own.shape[1]
    pieces = flat.shape[1]
    part = own.shape[3]
    scale = 1.0 / math.sqrt(HD)

    x_copies = [
        pltpu.make_async_copy(x, x_here.at[s], x_sem.at[s])
        for s, x in enumerate((x_first, x_second))
    ]

    def in_copy(b):
        return pltpu.make_async_copy(
            w_in.at[:, pl.ds(pl.multiple_of(b * cw, cw), cw)], weights.at[b], in_sem.at[b]
        )

    def out_copy(n, p):
        return pltpu.make_async_copy(
            w_out.at[
                pl.ds(p * depth, depth), pl.ds(pl.multiple_of(n * cw, cw), cw)
            ],
            weights.at[n * pieces + p],
            out_sem.at[n],
        )

    def out_ready(n):
        ref = weights.at[pl.ds(n * pieces, pieces)]
        return pltpu.make_async_copy(ref, ref, out_sem.at[n])

    kv_copies = [
        pltpu.make_async_copy(keys, k_here.at[:, pl.ds(0, slots)], kv_sem.at[0]),
        pltpu.make_async_copy(values, v_here.at[:, pl.ds(0, slots)], kv_sem.at[1]),
    ]

    def send_sq():
        return remote(sq.at[:, 1 - side], sq_other, sq_send, sq_recv, other)

    def send_sq_along(d):
        return remote(sq_to.at[d], sq_along.at[d], sqa_send, sqa_recv, along[d])

    def send_pair(n):
        return remote(
            prod.at[n, :, 1 - side], from_other.at[n], pair_send, pair_recv.at[n], other
        )

    def send_along(n, f, d):
        return remote(
            to_along.at[n, f, d], from_along.at[n, f, d],
            along_send.at[f], along_recv.at[n, f], along[d],
        )

    def send_across(n, f, d):
        return remote(
            to_across.at[n, f, lax.rem(gy + d + 1, inner)], joined.at[gy, n, f],
            across_send.at[f], across_recv.at[f], across[d],
        )

    def keep_own(n, f):
        return pltpu.make_async_copy(
            to_across.at[n, f, gy], joined.at[gy, n, f], own_sem.at[f]
        )

    def source(d):
        return lax.rem(gy + inner - d, inner)

    def send_rows(f, d):
        return remote(
            to_rows.at[f, d], held.at[f, gx, gy], rows_send.at[f], rows_recv.at[f, d], across[d]
        )

    def keep_rows(f):
        return pltpu.make_async_copy(
            to_rows.at[f, inner - 1], held.at[f, gx, gy], keep_sem.at[f]
        )

    def gather(f, d, e):
        ref = held.at[f, gx, source(d)]
        origin = to_rows.at[f, inner - 1] if d == 0 else ref
        return remote(origin, ref, gather_send.at[f], gather_recv.at[f, e], along[e])

    def share(f, e):
        ref = held.at[f, 2 * lax.rem(pair + pairs - e, pairs) + side]
        return remote(ref, ref, share_send.at[f], share_recv.at[f, e], other)

    def send_sum(f, n, d):
        return remote(
            to_sum.at[f, n, d], from_sum.at[f, n, d],
            sum_send.at[f], sum_recv.at[f, n], across[d],
        )

    relays = relays_of(inner, out_blocks)
    near = gy + 1 - 2 * lax.rem(gy, 2)
    near_far, far = lax.rem(near + 2, inner), lax.rem(gy + 2, inner)

    def relay_index(f, n):
        return sum(relays[:f]) + n

    def send_near(k):
        return remote(to_near.at[k], from_near.at[k], near_send, near_recv.at[k], (gx, near))

    def send_wide(k):
        return remote(wide_near.at[k], wide_from.at[k], wide_send, wide_recv.at[k], (gx, near))

    def send_far(k):
        return remote(to_far.at[k], from_far.at[k], far_send, far_recv.at[k], (gx, far))

    def arrived(ref, sem):
        pltpu.make_async_copy(ref, ref, sem).wait()

    for copy in x_copies:
        copy.start()

    @pl.loop(0, chunks)
    def _(b):
        in_copy(b).start()

    for copy in kv_copies:
        copy.start()

    barrier = pltpu.get_barrier_semaphore()
    peers = [other] + along + across
    for peer in peers:
        pl.semaphore_signal(barrier, inc=1, device_id=peer, device_id_type=MESH)

    to = lax.broadcasted_iota(jnp.int32, (here, here), 0)
    step = lax.rem(lax.div(to, half_rows), STEPS)
    member = lax.rem(lax.div(to, tile), inner)
    start = lax.div(to, half) * half_rows + lax.rem(to, half_rows)
    source_row = step * block + member * rows + start
    order = jnp.where(
        source_row == lax.broadcasted_iota(jnp.int32, (here, here), 1), 1.0, 0.0
    ).astype(jnp.bfloat16)
    wide_gain = gain[...].astype(jnp.float32).reshape(1, depth)
    for copy in x_copies:
        copy.wait()

    @pl.loop(0, outer)
    def _(g):
        parts = []
        for s in range(STEPS):
            wide = x_here[s, pl.ds(pl.multiple_of(g * block, block), block), :].astype(jnp.float32)
            parts.append((wide * wide_gain).astype(jnp.bfloat16))
            total = jnp.sum(wide * wide, axis=1, keepdims=True)
            sq[g // 2, lax.rem(g, 2), s * block : (s + 1) * block, :] = jnp.broadcast_to(
                total, (block, HD)
            )
        scaled[pl.ds(pl.multiple_of(g * here, here), here), :] = jnp.dot(
            order, jnp.concatenate(parts, axis=0), preferred_element_type=jnp.float32
        ).astype(jnp.bfloat16)

    pl.semaphore_wait(barrier, len(peers))
    send_sq().start()

    def pass_on(n):
        send_pair(n).wait_recv()
        for d in range(pairs - 1):
            there = lax.rem(pair + d + 1, pairs)
            both = (prod[n, there, side] + from_other[n, there]).astype(jnp.bfloat16)
            for f in range(HALVES):
                to_along[n, f, d] = both[f * half : (f + 1) * half]
            send_along(n, 0, d).start()

    @pl.loop(0, chunks)
    def _(n):
        in_copy(n).wait()
        product = jnp.dot(scaled[...], weights[n], preferred_element_type=jnp.float32)
        prod[n] = product.reshape(pairs, 2, here, cw)
        send_pair(n).start()

        @pl.when(n == 0)
        def _():
            send_sq().wait()
            for d in range(pairs - 1):
                there = lax.rem(pair + d + 1, pairs)
                sq_to[d] = sq[there, side] + sq_other[there]
                send_sq_along(d).start()

        @pl.when(n >= LAG)
        def _():
            pass_on(n - LAG)

    @pl.loop(chunks - LAG, chunks)
    def _(n):
        pass_on(n)

    @pl.loop(0, chunks)
    def _(n):
        for f in range(1, HALVES):
            for d in range(pairs - 1):
                send_along(n, f, d).start()

    @pl.loop(0, out_blocks)
    def _(n):
        for p in range(pieces):
            out_copy(n, p).start()

    squares = sq[pair, side] + sq_other[pair]
    arrived(sq_along, sqa_recv)
    for d in range(pairs - 1):
        squares = squares + sq_along[d]
    factor = lax.rsqrt(squares / width + norm_eps)
    for f in range(HALVES):
        for z in range(inner):
            for s in range(STEPS):
                target = f * half + z * tile + s * half_rows
                row = s * block + z * rows + f * half_rows
                sq[0, 0, target : target + half_rows, :] = factor[row : row + half_rows]

    index = lax.rem(lax.broadcasted_iota(jnp.int32, (SUB, HD), 0), tile)
    lane = lax.broadcasted_iota(jnp.int32, (SUB, HD), 1)
    cosines, sines = [], []
    for f in range(HALVES):
        position = jnp.zeros((SUB, HD), jnp.float32)
        for s in range(STEPS):
            for i in range(half_rows):
                position = jnp.where(
                    index == s * half_rows + i,
                    (lengths[f * half_rows + i] + s).astype(jnp.float32),
                    position,
                )
        angle = position * freq[...]
        cosines.append(jnp.cos(angle))
        sines.append(jnp.where(lane < HD // 2, -jnp.sin(angle), jnp.sin(angle)))

    def settle(n, f):
        arrived(from_along.at[n, f], along_recv.at[n, f])
        span = slice(f * half, (f + 1) * half)
        for h in range(chunk_heads):
            columns = slice(h * HD, (h + 1) * HD)
            total = prod[n, pair, side, span, columns] + from_other[n, pair, span, columns]
            for d in range(pairs - 1):
                total = total + from_along[n, f, d, :, columns].astype(jnp.float32)
            total = total * sq[0, 0, span, :]
            for z in range(inner):
                mixed[z, h * tile : (h + 1) * tile, :] = total[z * tile : (z + 1) * tile]
        for z in range(inner):
            to_across[n, f, z] = (
                mixed[z].reshape(chunk_heads // per_tile, SUB, HD).astype(jnp.bfloat16)
            )
        for d in range(inner - 1):
            send_across(n, f, d).start()
        keep_own(n, f).start()

    early = chunks // 2

    @pl.loop(0, chunks)
    def _(n):
        settle(n, 0)

    @pl.loop(0, early)
    def _(n):
        settle(n, 1)

    upper = lax.broadcasted_iota(jnp.int32, (SUB, HD), 0) < tile
    queries = size // per_tile
    kv_heads = inner * groups
    columns = kv_heads * STEPS * size
    slot = lax.broadcasted_iota(jnp.int32, (slots + EXTRA, columns), 0)
    column = lax.broadcasted_iota(jnp.int32, (1, columns), 1)
    newest = jnp.where(lax.rem(column, STEPS * size) >= size, slots + 1, slots)

    def forward(f, d):
        for e in range(pairs - 1):
            gather(f, d, e).start()

    def forward_all(f):
        for d in range(1, inner):
            send_rows(f, d - 1).wait_recv()
            forward(f, d)
        keep_rows(f).wait()
        share(f, 0).start()

    fresh[...] = jnp.zeros_like(fresh)

    @pl.loop(0, half_rows)
    def _(i):
        spread[i] = jnp.zeros(spread.shape[1:], jnp.bfloat16)

    for copy in kv_copies:
        copy.wait()

    for f in range(HALVES):

        @pl.loop(0, chunks)
        def _(n):
            if f > 0:

                @pl.when(n >= early)
                def _():
                    settle(n, f)

        if f > 0:
            forward_all(f - 1)
        arrived(joined.at[0, :, f], own_sem.at[f])
        arrived(joined.at[pl.ds(0, inner - 1), :, f], across_recv.at[f])

        @pl.loop(0, inner)
        def _(y):
            here_now = joined[y, :, f].reshape(groups * per * tile // SUB, SUB, HD)
            for j in range(groups):
                k = y * groups + j
                turn = here_now[j * per * tile // SUB : (j + 1) * per * tile // SUB]
                turn = turn.astype(jnp.float32)
                turned_now = turn * cosines[f][None] + pltpu.roll(turn, HD // 2, 2) * sines[f][None]
                turned_now = turned_now.astype(jnp.bfloat16).astype(jnp.float32)
                turned[j, : size * tile] = turned_now[:queries].reshape(size * tile, HD)
                turned[j, size * tile :] = jnp.where(upper, turned_now[queries], turn[queries])
                place = pl.ds(pl.multiple_of(k * HD, HD), HD)
                band = pl.ds(pl.multiple_of(k * STEPS * size, STEPS * size), STEPS * size)
                for i in range(half_rows):
                    query = jnp.concatenate(
                        [
                            turned[j, pl.ds(s * half_rows + i, size, stride=tile), :]
                            for s in range(STEPS)
                        ],
                        axis=0,
                    )
                    spread[i, band, place] = query.astype(jnp.bfloat16)
                    for s in range(STEPS):
                        for c in range(2):
                            row = (size + c) * tile + s * half_rows + i
                            fresh[i, c, s : s + 1, place] = turned[j, row : row + 1, :]

        for i in range(half_rows):
            row = f * half_rows + i
            k_here[row, slots:, :] = fresh[i, 0].astype(jnp.bfloat16)
            v_here[row, slots:, :] = fresh[i, 1].astype(jnp.bfloat16)
            scores = (
                lax.dot_general(
                    k_here[row],
                    spread[i],
                    (((1,), (1,)), ((), ())),
                    preferred_element_type=jnp.float32,
                )
                * scale
            )
            valid = (slot < lengths[row]) | ((slot >= slots) & (slot <= newest))
            scores = jnp.where(valid, scores, -jnp.inf)
            soft = jnp.exp(scores - jnp.max(scores, axis=0, keepdims=True))
            total = jnp.sum(soft, axis=0, keepdims=True)
            total = jnp.broadcast_to(total, (SUB, columns)).T
            soft = soft.astype(jnp.bfloat16).T
            for k in range(kv_heads):
                band = slice(k * STEPS * size, (k + 1) * STEPS * size)
                blend = jnp.dot(
                    soft[band],
                    v_here[row, :, k * HD : (k + 1) * HD],
                    preferred_element_type=jnp.float32,
                )
                blend = blend / total[band, 0:1]
                for s in range(STEPS):
                    mix[k, pl.ds(s * half_rows + i, size, stride=tile), :] = blend[
                        s * size : (s + 1) * size
                    ]

        for d in range(inner):
            there = lax.rem(gy + d + 1, inner)
            for j in range(groups):
                to_rows[f, d, j] = (
                    mix[there * groups + j].reshape(queries, SUB, HD).astype(jnp.bfloat16)
                )
            if d < inner - 1:
                send_rows(f, d).start()
        keep_rows(f).start()
        forward(f, 0)

    heads_piece = depth // HD
    span = inner * tile

    def pass_side(f):
        for e in range(pairs - 1):
            arrived(held.at[f, 0], gather_recv.at[f, e])
            share(f, e + 1).start()

    def bring(f):
        fill(f, side)
        for e in range(pairs):
            share(f, e).wait_recv()
        fill(f, 1 - side)

    def fill(f, which):
        @pl.loop(0, pairs)
        def _(c):
            g = 2 * c + which
            place = pl.ds(pl.multiple_of(g * span, span), span)
            for j in range(groups):
                for q in range(queries):
                    both = held[f, g, :, j, q].astype(jnp.float32)
                    for t in range(per_tile):
                        for z in range(inner):
                            parted[q, t, z * tile : (z + 1) * tile, :] = both[
                                z, t * tile : (t + 1) * tile
                            ]
                    for t in range(per_tile):
                        head = j * size + q * per_tile + t
                        column = (head % heads_piece) * HD
                        flat[f, head // heads_piece, place, column : column + HD] = parted[
                            q, t
                        ].astype(jnp.bfloat16)

    def relay_on(f):
        if relays[f]:

            @pl.loop(0, relays[f])
            def _(n):
                k = relay_index(f, n)
                send_wide(k).wait_recv()
                to_far[k] = (own[f, n, far] + wide_from[k]).astype(jnp.bfloat16)
                send_far(k).start()

    for f in range(HALVES):
        if f < HALVES - 1:
            pass_side(f)
        if f == max(HALVES - 2, 0):
            forward_all(HALVES - 1)
        if f == HALVES - 1:
            pass_side(f)
            relay_on(f - 1)
        bring(f)

        def multiply(n):
            total = None
            if f == 0:
                out_ready(n).wait()
            for p in range(pieces):
                product = jnp.dot(
                    flat[f, p], weights[n * pieces + p], preferred_element_type=jnp.float32
                )
                total = product if total is None else total + product
            own[f, n] = total.reshape(inner, part, cw)

        if relays[f]:

            @pl.loop(0, relays[f])
            def _(n):
                multiply(n)
                k = relay_index(f, n)
                wide_near[k] = own[f, n, near_far]
                send_wide(k).start()
                to_near[k] = own[f, n, near].astype(jnp.bfloat16)
                send_near(k).start()

        @pl.loop(relays[f], out_blocks)
        def _(n):
            multiply(n)
            for d in range(inner - 1):
                to_sum[f, n, d] = own[f, n, lax.rem(gy + d + 1, inner)].astype(jnp.bfloat16)
                send_sum(f, n, d).start()

        if f == HALVES - 1:
            relay_on(f)

    for f in range(HALVES):

        def settle_sum(n, terms):
            for c in range(cw // HD):
                columns = slice(c * HD, (c + 1) * HD)
                total = own[f, n, gy, :, columns]
                for term in terms:
                    total = total + term[:, columns].astype(jnp.float32)
                place = pl.ds(pl.multiple_of(n * cw + c * HD, HD), HD)
                for q in range(part // tile):
                    for s in range(STEPS):
                        start = q * tile + s * half_rows
                        target = q * rows + f * half_rows
                        piece[s, target : target + half_rows, place] = total[
                            start : start + half_rows
                        ]
                if f == HALVES - 1:
                    for s in range(STEPS):
                        result[s, :, place] = piece[s, :, place].astype(jnp.bfloat16)

        if relays[f]:

            @pl.loop(0, relays[f])
            def _(n):
                k = relay_index(f, n)
                send_near(k).wait_recv()
                send_far(k).wait_recv()
                settle_sum(n, [from_near.at[k], from_far.at[k]])

        @pl.loop(relays[f], out_blocks)
        def _(n):
            arrived(from_sum.at[f, n], sum_recv.at[f, n])
            settle_sum(n, [from_sum.at[f, n, d] for d in range(inner - 1)])

    arrived(prod.at[:, :, 0], pair_send)
    arrived(sq_to, sqa_send)
    for f in range(HALVES):
        arrived(to_along.at[:, f], along_send.at[f])
        arrived(to_across.at[:, f, pl.ds(0, inner - 1)], across_send.at[f])
        arrived(to_rows.at[f, pl.ds(0, inner - 1)], rows_send.at[f])
        arrived(held.at[f, pl.ds(0, pairs - 1)], gather_send.at[f])
        arrived(held.at[f, pl.ds(0, pairs)], share_send.at[f])
        arrived(to_sum.at[f, pl.ds(relays[f], out_blocks - relays[f])], sum_send.at[f])
    if sum(relays):
        arrived(to_near, near_send)
        arrived(wide_near, wide_send)
        arrived(to_far, far_send)


def body(x_first, x_second, norm_gain, w_qkv, w_out, cache_keys, cache_values, lengths):
    outer, inner = lax.axis_size("gx"), lax.axis_size("gy")
    rows, slots, kv_width = cache_keys.shape
    depth, in_columns = w_qkv.shape
    out_depth, out_columns = w_out.shape
    width = depth * outer
    heads = in_columns // HD
    groups = kv_width // HD // inner
    size = heads // groups - 2
    chunk_heads = 4 if in_columns % (4 * HD) == 0 and out_columns % (4 * HD) == 0 else 2
    chunks = heads // chunk_heads
    cw = chunk_heads * HD
    pairs = outer // 2
    here = STEPS * inner * rows
    tile = STEPS * rows // HALVES
    queries = size * tile // SUB
    total = outer * here // HALVES
    part = total // inner
    out_blocks = out_columns // cw
    pieces = out_depth // depth
    relayed = max(1, sum(relays_of(inner, out_blocks)))
    dims = (outer, inner, rows, width, groups, size, chunk_heads, chunks)

    half = HD // 2
    freq = rotary_base ** (-(np.arange(half, dtype=np.float64) * 2.0 / HD))
    freq = jnp.asarray(np.tile(freq, 2)[None], jnp.float32)

    dma = pltpu.SemaphoreType.DMA
    vmem = pl.BlockSpec(memory_space=pltpu.VMEM)
    away = pl.BlockSpec(memory_space=pl.ANY)
    f32, b16 = jnp.float32, jnp.bfloat16
    result = pl.pallas_call(
        functools.partial(block_kernel, dims),
        in_specs=[
            pl.BlockSpec(memory_space=pltpu.SMEM), away, away, vmem, vmem, away, away, away, away,
        ],
        out_specs=vmem,
        out_shape=pltpu.VMEM((STEPS, HALVES * part // STEPS, out_columns), b16),
        scratch_shapes=[
            pltpu.VMEM((STEPS, outer * inner * rows, depth), b16),
            pltpu.VMEM((rows, slots + EXTRA, kv_width), b16),
            pltpu.VMEM((rows, slots + EXTRA, kv_width), b16),
            pltpu.VMEM((max(in_columns // cw, out_blocks * pieces), depth, cw), b16),
            pltpu.VMEM((outer * here, depth), b16),
            pltpu.VMEM((chunks, pairs, 2, here, cw), f32),
            pltpu.VMEM((chunks, pairs, here, cw), f32),
            pltpu.VMEM((chunks, HALVES, pairs - 1, here // HALVES, cw), b16),
            pltpu.VMEM((chunks, HALVES, pairs - 1, here // HALVES, cw), b16),
            pltpu.VMEM((pairs, 2, here, HD), f32),
            pltpu.VMEM((pairs, here, HD), f32),
            pltpu.VMEM((pairs - 1, here, HD), f32),
            pltpu.VMEM((pairs - 1, here, HD), f32),
            pltpu.VMEM((inner, chunk_heads * tile, HD), f32),
            pltpu.VMEM((chunks, HALVES, inner, chunk_heads * tile // SUB, SUB, HD), b16),
            pltpu.VMEM((inner, chunks, HALVES, chunk_heads * tile // SUB, SUB, HD), b16),
            pltpu.VMEM((groups, (size + 2) * tile, HD), f32),
            pltpu.VMEM((rows // HALVES, kv_width // HD * STEPS * size, kv_width), b16),
            pltpu.VMEM((rows // HALVES, 2, EXTRA, kv_width), f32),
            pltpu.VMEM((kv_width // HD, size * tile, HD), f32),
            pltpu.VMEM((HALVES, inner, groups, queries, SUB, HD), b16),
            pltpu.VMEM((HALVES, outer, inner, groups, queries, SUB, HD), b16),
            pltpu.VMEM((queries, SUB // tile, inner * tile, HD), f32),
            pltpu.VMEM((HALVES, pieces, total, depth), b16),
            pltpu.VMEM((HALVES, out_blocks, inner, part, cw), f32),
            pltpu.VMEM((HALVES, out_blocks, inner - 1, part, cw), b16),
            pltpu.VMEM((HALVES, out_blocks, inner - 1, part, cw), b16),
            pltpu.VMEM((STEPS, HALVES * part // STEPS, out_columns), f32),
            pltpu.VMEM((relayed, part, cw), b16),
            pltpu.VMEM((relayed, part, cw), b16),
            pltpu.VMEM((relayed, part, cw), f32),
            pltpu.VMEM((relayed, part, cw), f32),
            pltpu.VMEM((relayed, part, cw), b16),
            pltpu.VMEM((relayed, part, cw), b16),
            dma((STEPS,)), dma((2,)), dma((chunks,)), dma((out_blocks,)),
            dma, dma((chunks,)),
            dma((HALVES,)), dma((chunks, HALVES)),
            dma((HALVES,)), dma((HALVES,)),
            dma, dma, dma, dma, dma((HALVES,)),
            dma((HALVES,)), dma((HALVES, inner - 1)), dma((HALVES,)),
            dma((HALVES,)), dma((HALVES, pairs - 1)),
            dma((HALVES,)), dma((HALVES, pairs)),
            dma((HALVES,)), dma((HALVES, out_blocks)),
            dma, dma((relayed,)), dma, dma((relayed,)), dma, dma((relayed,)),
        ],
        compiler_params=pltpu.CompilerParams(
            collective_id=0, has_side_effects=True, vmem_limit_bytes=VMEM_LIMIT
        ),
        name="decode_block",
    )(lengths, x_first, x_second, norm_gain, freq, w_qkv, w_out, cache_keys, cache_values)
    return result[0], result[1]


def solution(mesh):
    in_specs = (
        P(None, "gx"),
        P(None, "gx"),
        P("gx"),
        P("gx", "gy"),
        P("gy", "gx"),
        P(("gx", "gy"), None, None),
        P(("gx", "gy"), None, None),
        P(("gx", "gy")),
    )
    out_specs = (P("gy", "gx"), P("gy", "gx"))
    return jax.shard_map(body, mesh=mesh, in_specs=in_specs, out_specs=out_specs, check_vma=False)
```
